256 devices in a mesh: dp: 16 (over z, y_lo), dep: 4 (over x), hgt: 4 (over y_hi, core).
Axes of the slice: x: 4, y: 4 (y_hi: 2, y_lo: 2; y = y_hi * 2 + y_lo), z: 8, core: 2. Of those that a mesh axis runs over, the one named last changes fastest.
Arguments:
- volume: bfloat16 [16, 32, 8, 32, 128], P('dp', None, 'dep', 'hgt'), may hold values from -6 to 6
- kernel_first: bfloat16 [27, 64, 32], replicated, may hold values from -0.21875 to 0.21875
- kernel_second: bfloat16 [27, 128, 64], replicated, may hold values from -0.15625 to 0.15625
- cotangent: bfloat16 [16, 128, 8, 32, 128], P('dp', None, 'dep', 'hgt'), may hold values from -0.01171875 to 0.01171875
Outputs:
- features: bfloat16 [16, 128, 8, 32, 128], P('dp', None, 'dep', 'hgt')
- grad_first: float32 [27, 64, 32], P(None, 'dp')
- grad_second: float32 [27, 128, 64], P(None, 'dp')
The draws below stay inside these ranges and needn't reach their ends.
All inputs are finite; a program needn't handle non-finite values.
Results may differ from the reference program's by a relative error of at most 0.0049.
Values may be sent and summed in bfloat16 or wider, within the bound.
A program may use at most 64 MiB of HBM per device.

```python
import jax
import jax.numpy as jnp

CH_IN = 32
CH_MID = 64
CH_OUT = 128
WIDTH = 128
VOLUMES = 16
DEPTH = 8
HEIGHT = 32


def with_spikes(drawn, stream_key, source, target, blocks, factor):
    owner, partner = [(jnp.arange(drawn.shape[position]) // (drawn.shape[position] // blocks)).reshape([-1 if axis == position else 1 for axis in range(drawn.ndim)]) for position in (source, target)]
    chosen = jax.random.permutation(stream_key, blocks)[partner]
    strong = (owner == chosen) | (owner == (partner + blocks // 2) % blocks)
    return jnp.where(strong, factor * drawn, drawn)


def level_of(stream_key, shape, split, least, largest):
    loudness, own = 1.0, jax.random.fold_in(stream_key, 6)
    for dim, shards_of in split:
        steps = jnp.exp(jax.random.uniform(jax.random.fold_in(own, dim), (shards_of,), jnp.float32, least / len(split), largest / len(split)))
        loudness = loudness * jnp.repeat(steps, shape[dim] // shards_of).reshape([-1 if axis == dim else 1 for axis in range(len(shape))])
    return loudness


def noise(key, dims, deviation, most, split=(), kind=jnp.bfloat16):
    drawn = jax.random.normal(key, dims, jnp.float32) * deviation
    if len(split) > 0:
        drawn = level_of(key, dims, split, -0.22, 0.18) * drawn
    return jnp.clip(drawn, min=-most, max=most).astype(kind)


def gaussian_with(key, extent, spread, most, split, heavy, dtype=jnp.bfloat16):
    values = spread * jax.random.normal(key, extent, jnp.float32)
    if split:
        values = values * level_of(key, extent, split, -0.22, 0.18)
    return jnp.clip(with_spikes(values, jax.random.fold_in(key, 3), *heavy), -most, most).astype(dtype)


def setup_inputs(seed: int = 0) -> dict:
    arg_keys = jax.random.split(jax.random.key(seed), 5)
    return {
        "volume": noise(arg_keys[0], (VOLUMES, CH_IN, DEPTH, HEIGHT, WIDTH), 1.0, 6.0, ((0, 16), (2, 4), (3, 4))),
        "kernel_first": noise(arg_keys[1], (27, CH_MID, CH_IN), (27 * CH_IN) ** -0.5, 0.21875),
        "kernel_second": noise(arg_keys[2], (27, CH_OUT, CH_MID), (27 * CH_MID) ** -0.5, 0.15625),
        "cotangent": gaussian_with(arg_keys[3], (VOLUMES, CH_OUT, DEPTH, HEIGHT, WIDTH), ((VOLUMES * DEPTH * HEIGHT * WIDTH) ** -0.5), 0.01171875, ((0, 16), (2, 4), (3, 4)), (0, 1, 16, 2.0)),
    }


OFFSETS = [(first, second, third) for first in (-1, 0, 1) for second in (-1, 0, 1) for third in (-1, 0, 1)]

def pad_all(field):
    return jnp.pad(field, ((0, 0), (0, 0), (1, 1), (1, 1), (1, 1)))

def window(padded, shift_d, shift_h, shift_w, depth, height, width):
    return padded[:, :, 1 + shift_d:1 + shift_d + depth, 1 + shift_h:1 + shift_h + height, 1 + shift_w:1 + shift_w + width]

def reference(volume, kernel_first, kernel_second, cotangent):
    depth, height, width = (volume.shape[2], volume.shape[3], volume.shape[4])

    def convolve(field, kernel):
        padded = pad_all(field).astype(jnp.float32)
        total = jnp.zeros((field.shape[0], kernel.shape[1], depth, height, width), jnp.float32)
        for number, shift in enumerate(OFFSETS):
            piece = window(padded, shift[0], shift[1], shift[2], depth, height, width)
            total = total + jnp.einsum('oi,bidhw->bodhw', kernel[number].astype(jnp.float32), piece)
        return total

    def kernel_grad(upstream, field):
        padded = pad_all(field).astype(jnp.float32)
        upper = upstream.astype(jnp.float32)
        parts = []
        for shift in OFFSETS:
            piece = window(padded, shift[0], shift[1], shift[2], depth, height, width)
            parts.append(jnp.einsum('bodhw,bidhw->oi', upper, piece))
        return jnp.stack(parts)
    pre = convolve(volume, kernel_first)
    hidden = jax.nn.silu(pre).astype(jnp.bfloat16)
    features = convolve(hidden, kernel_second).astype(jnp.bfloat16)
    grad_second = kernel_grad(cotangent, hidden)
    padded_cot = pad_all(cotangent).astype(jnp.float32)
    back = jnp.zeros(pre.shape, jnp.float32)
    for number, shift in enumerate(OFFSETS):
        piece = window(padded_cot, -shift[0], -shift[1], -shift[2], depth, height, width)
        back = back + jnp.einsum('oi,bodhw->bidhw', kernel_second[number].astype(jnp.float32), piece)
    sigma = jax.nn.sigmoid(pre)
    delta = (back * (sigma * (1.0 + pre * (1.0 - sigma)))).astype(jnp.bfloat16)
    grad_first = kernel_grad(delta, volume)
    return (features, grad_first, grad_second)
```

```python
import functools

import jax
import jax.numpy as jnp
from jax import lax
from jax.experimental import pallas as pl
from jax.experimental.pallas import tpu as pltpu
from jax.sharding import PartitionSpec as P

MESH = pl.DeviceIdType.MESH
BF = jnp.bfloat16
F32 = jnp.float32
W = 128
DIRS = [(a, b) for a in (-1, 0, 1) for b in (-1, 0, 1) if (a, b) != (0, 0)]
NT = (((1,), (1,)), ((), ()))


def dot(a, b):
    return jnp.dot(a, b, preferred_element_type=F32)


def shifted(x, by):
    if by == 0:
        return x
    lane = lax.broadcasted_iota(jnp.int32, x.shape, 1)
    keep = lane >= by if by > 0 else lane < W + by
    return jnp.where(keep, pltpu.roll(x, by % W, 1), 0.0)


def pair(ref, d, h, rows):
    halves = [ref[d + e, pl.ds(h, 3)].reshape(rows, W) for e in (0, 1)]
    return jnp.concatenate(halves, axis=1)


def kernel(
    sizes,
    vol,
    k1t,
    k2t,
    cot,
    feat,
    g1_out,
    g2_out,
    V,
    C,
    tmp,
    W1,
    W2,
    WB,
    BS,
    BO,
    RBX,
    RBH,
    RBD,
    H,
    H3,
    DS,
    D3,
    G,
    GB,
    RC,
    ZS,
    RZ,
    RY,
    RX,
    FS,
    FO,
    v_send,
    v_recv,
    b_send,
    b_recv,
    c_send,
    c_recv,
    z_send,
    z_recv,
    y_send,
    y_recv,
    x_send,
    x_recv,
    f_send,
    f_recv,
):
    n_z, n_y, n_dep, n_hgt = sizes
    rows = 128 // n_z
    dp, dep, hgt = (lax.axis_index(name) for name in ("dp", "dep", "hgt"))
    z, yl = dp // 2, dp % 2
    yh, core = hgt // 2, hgt % 2
    y = yh * 2 + yl

    def there(direction, sign):
        d, h = dep + sign * direction[0], hgt + sign * direction[1]
        return (d >= 0) & (d < n_dep) & (h >= 0) & (h < n_hgt)

    def z_peer(m):
        return (((z + m) % n_z) * 2 + yl, dep, hgt)

    def y_peer(m):
        other = (y + m) % n_y
        return (z * 2 + other % 2, dep, (other // 2) * 2 + core)

    def x_peer(m):
        return (dp, (dep + m) % n_dep, hgt)

    partner = (dp, dep, hgt + 1 - 2 * core)

    V[...] = jnp.zeros_like(V)
    RBX[...] = jnp.zeros_like(RBX)
    RBH[...] = jnp.zeros_like(RBH)
    RBD[...] = jnp.zeros_like(RBD)

    barrier = pltpu.get_barrier_semaphore()
    for direction in DIRS:

        @pl.when(there(direction, 1))
        def _():
            pl.semaphore_signal(
                barrier,
                inc=1,
                device_id=(dp, dep + direction[0], hgt + direction[1]),
                device_id_type=MESH,
            )

    peers = [partner]
    peers += [z_peer(m) for m in range(1, n_z)]
    peers += [y_peer(m) for m in range(1, n_y)]
    peers += [x_peer(m) for m in range(1, n_dep)]
    for peer in peers:
        pl.semaphore_signal(barrier, inc=1, device_id=peer, device_id_type=MESH)

    for d in (0, 1):
        tmp[0:256, :] = vol[:, d].astype(F32).reshape(256, W)
        for h in range(8):
            V[2 + d, 2 + h] = tmp[pl.ds(h, 32, stride=8), :].astype(BF)

    span_d = 1 + (dep > 0).astype(jnp.int32) + (dep < n_dep - 1).astype(jnp.int32)
    span_h = 1 + (hgt > 0).astype(jnp.int32) + (hgt < n_hgt - 1).astype(jnp.int32)
    pl.semaphore_wait(barrier, span_d * span_h - 1 + len(peers))

    def v_copy(k):
        a, b = DIRS[k]
        to_d = {0: (2, 4), 1: (0, 2), -1: (4, 6)}[a]
        from_h, to_h = {0: ((2, 10), (2, 10)), 1: ((8, 10), (0, 2)), -1: ((2, 4), (10, 12))}[b]
        return pltpu.make_async_remote_copy(
            src_ref=V.at[2:4, from_h[0] : from_h[1]],
            dst_ref=V.at[to_d[0] : to_d[1], to_h[0] : to_h[1]],
            send_sem=v_send.at[k],
            recv_sem=v_recv.at[k],
            device_id=(dp, dep + a, hgt + b),
            device_id_type=MESH,
        )

    def b_copy(k):
        a, b = DIRS[k]
        d = {-1: 0, 1: 3}.get(a)
        h = {-1: 0, 1: 9}.get(b)
        if a == 0:
            src, dst = BS.at[1:3, h], RBH.at[(b + 1) // 2]
        elif b == 0:
            src, dst = BS.at[d, 1:9], RBX.at[(a + 1) // 2]
        else:
            src, dst = BS.at[d, h], RBD.at[(a + 1) + (b + 1) // 2]
        return pltpu.make_async_remote_copy(
            src_ref=src,
            dst_ref=dst,
            send_sem=b_send.at[k],
            recv_sem=b_recv.at[k],
            device_id=(dp, dep + a, hgt + b),
            device_id_type=MESH,
        )

    def halo(copy, sign, what):
        for k, direction in enumerate(DIRS):

            @pl.when(there(direction, sign))
            def _():
                getattr(copy(k), what)()

    halo(v_copy, 1, "start")

    for d in (0, 1):
        for h in (0, 1, 10, 11):
            C[d, h] = jnp.zeros((128, W), BF)
        tmp[...] = cot[:, d].astype(F32).reshape(1024, W)

        @pl.loop(0, 8)
        def _(h):
            C[d, 2 + h] = tmp[pl.ds(h, 128, stride=8), :].astype(BF)

    for a in range(3):
        for b in range(3):
            for c in range(3):
                WB[a * 192 + c * 64 : a * 192 + c * 64 + 64, (2 - b) * 128 : (3 - b) * 128] = k2t[
                    9 * a + 3 * b + c
                ]

    @pl.loop(0, 10)
    def _(h):
        t = dot(WB[...], pair(C, 0, h, 384))
        sums = []
        for a in range(3):
            halves = []
            for e in (0, 1):
                parts = [
                    shifted(t[a * 192 + c * 64 : a * 192 + c * 64 + 64, e * W : e * W + W], c - 1)
                    for c in range(3)
                ]
                halves.append(parts[0] + parts[1] + parts[2])
            sums.append(halves)
        inner = [sums[0][1] + sums[1][0], sums[1][1] + sums[2][0]]
        BS[0, h] = sums[0][0].astype(BF)
        BS[3, h] = sums[2][1].astype(BF)
        for d in (0, 1):
            BS[1 + d, h] = inner[d].astype(BF)
            BO[d, h] = inner[d]

    halo(b_copy, 1, "start")

    for c in range(3):
        stack = [k1t[3 * t + c].astype(F32) for t in range(9)]
        W1[c * 64 : c * 64 + 64, :] = jnp.concatenate(stack, axis=0).T.astype(BF)

    halo(v_copy, -1, "wait_recv")

    @pl.loop(0, 10)
    def _(h):
        ok_h = ((h > 0) | (hgt > 0)) & ((h < 9) | (hgt < n_hgt - 1))
        for d in (0, 2):
            x = jnp.concatenate([pair(V, d + a, h, 96) for a in range(3)], axis=0)
            t = dot(W1[...], x)
            for e in (0, 1):
                part = [t[c * 64 : c * 64 + 64, e * W : e * W + W] for c in range(3)]
                pre = shifted(part[0], 1) + part[1] + shifted(part[2], -1)
                sigma = 1.0 / (1.0 + jnp.exp(-pre))
                ok = ok_h
                if d + e == 0:
                    ok = ok & (dep > 0)
                elif d + e == 3:
                    ok = ok & (dep < n_dep - 1)
                hid = pre * sigma * ok.astype(F32)
                H[d + e, h] = hid.astype(BF)
                for c in range(3):
                    H3[d + e, h, c * 64 : c * 64 + 64] = shifted(hid, 1 - c).astype(BF)
                if d + e in (1, 2):
                    DS[d + e - 1, h] = sigma * (1.0 + pre * (1.0 - sigma))

    def keep(owner, unit, value):
        value = value.reshape(n_z, rows, W)
        G[owner, :, unit] = value
        GB[owner, :, unit] = value.astype(BF)

    upstream = [C[d, 2 + h] for h in range(8) for d in (0, 1)]
    upstream = jnp.concatenate(upstream, axis=1)
    lasts = {}
    for a in range(3):
        for b in range(3):
            field = [H3[d + a, h + b] for h in range(8) for d in (0, 1)]
            part = lax.dot_general(
                upstream, jnp.concatenate(field, axis=1), NT, preferred_element_type=F32
            )
            keep(0, 3 * a + b, part[:, :128])
            lasts[a, b] = part[:, 128:192]
        keep(1, a, jnp.concatenate([lasts[a, 0], lasts[a, 1]], axis=1))
    keep(1, 3, jnp.concatenate([lasts[0, 2], lasts[1, 2]], axis=1))
    keep(1, 4, jnp.concatenate([lasts[2, 2], jnp.zeros((128, 64), F32)], axis=1))

    halo(b_copy, -1, "wait_recv")

    for d, a in ((0, 1), (1, -1)):
        for h, b in ((0, 1), (7, -1)):
            BO[d, 1 + h] += RBH[(b + 1) // 2, d].astype(F32) + RBD[(a + 1) + (b + 1) // 2].astype(F32)

    @pl.loop(0, 8)
    def _(h):
        for d, a in ((0, 1), (1, -1)):
            back = BO[d, 1 + h] + RBX[(a + 1) // 2, h].astype(F32)
            delta = back * DS[d, 1 + h]
            for c in range(3):
                D3[2 * h + d, c * 64 : c * 64 + 64] = shifted(delta, c - 1).astype(BF)

    upstream = jnp.concatenate([D3[r] for r in range(16)], axis=1)
    field = [
        jnp.concatenate(
            [V[2 + d + a - 1, 2 + h - 1 : 2 + h + 2].reshape(96, W) for a in range(3)], axis=0
        )
        for h in range(8)
        for d in (0, 1)
    ]
    part = lax.dot_general(
        upstream, jnp.concatenate(field, axis=1), NT, preferred_element_type=F32
    )
    blocks = [part[c * 64 : c * 64 + 64, j * W : j * W + W] for c in range(3) for j in (0, 1)]
    ends = [part[c * 64 : c * 64 + 64, 256:288] for c in range(3)]
    blocks.append(jnp.concatenate(ends + [jnp.zeros((64, 32), F32)], axis=1))
    blocks.append(jnp.zeros((64, W), F32))
    for m in range(4):
        two = [blocks[2 * m + e].reshape(n_z, rows // 2, W) for e in (0, 1)]
        value = jnp.concatenate(two, axis=1)
        G[1, :, 5 + m] = value
        GB[1, :, 5 + m] = value.astype(BF)

    c_copy = pltpu.make_async_remote_copy(
        src_ref=GB.at[1 - core],
        dst_ref=RC,
        send_sem=c_send,
        recv_sem=c_recv,
        device_id=partner,
        device_id_type=MESH,
    )
    c_copy.start()
    for c in range(3):
        stack = [k2t[3 * t + c].astype(F32) for t in range(9)]
        W2[c * 128 : c * 128 + 128, :] = jnp.concatenate(stack, axis=0).T.astype(BF)
    c_copy.wait()

    @pl.loop(0, n_z)
    def _(j):
        ZS[j] = (G[core, j] + RC[j].astype(F32)).astype(BF)

    def z_copy(m):
        return pltpu.make_async_remote_copy(
            src_ref=ZS.at[(z + m) % n_z],
            dst_ref=RZ.at[m],
            send_sem=z_send.at[m],
            recv_sem=z_recv.at[m],
            device_id=z_peer(m),
            device_id_type=MESH,
        )

    for m in range(1, n_z):
        z_copy(m).start()

    @pl.loop(0, 8)
    def _(h):
        x = jnp.concatenate([pair(H, a, h, 192) for a in range(3)], axis=0)
        t = dot(W2[...], x)
        for d in (0, 1):
            part = [t[c * 128 : c * 128 + 128, d * W : d * W + W] for c in range(3)]
            total = shifted(part[0], 1) + part[1] + shifted(part[2], -1)
            FO[d, pl.ds(h, 128, stride=8), :] = total

    for d in (0, 1):
        feat[:, d] = FO[d].reshape(128, 8, W).astype(BF)

    for m in range(1, n_z):
        z_copy(m).wait()
    total = G[core, z] + RC[z].astype(F32)
    for m in range(1, n_z):
        total = total + RZ[m].astype(F32)
    RY[y] = total.astype(BF)

    def y_copy(m):
        return pltpu.make_async_remote_copy(
            src_ref=RY.at[y],
            dst_ref=RY.at[y],
            send_sem=y_send.at[m],
            recv_sem=y_recv.at[m],
            device_id=y_peer(m),
            device_id_type=MESH,
        )

    def y_wait(m):
        other = (y + n_y - m) % n_y
        return pltpu.make_async_remote_copy(
            src_ref=RY.at[y],
            dst_ref=RY.at[other],
            send_sem=y_send.at[m],
            recv_sem=y_recv.at[m],
            device_id=y_peer(m),
            device_id_type=MESH,
        )

    for m in range(1, n_y):
        y_copy(m).start()
    for m in range(1, n_y):
        y_wait(m).wait()
    total = RY[0].astype(F32)
    for m in range(1, n_y):
        total = total + RY[m].astype(F32)
    RX[dep] = total.astype(BF)

    def x_copy(m):
        return pltpu.make_async_remote_copy(
            src_ref=RX.at[dep],
            dst_ref=RX.at[dep],
            send_sem=x_send.at[m],
            recv_sem=x_recv.at[m],
            device_id=x_peer(m),
            device_id_type=MESH,
        )

    def x_wait(m):
        other = (dep + n_dep - m) % n_dep
        return pltpu.make_async_remote_copy(
            src_ref=RX.at[dep],
            dst_ref=RX.at[other],
            send_sem=x_send.at[m],
            recv_sem=x_recv.at[m],
            device_id=x_peer(m),
            device_id_type=MESH,
        )

    for m in range(1, n_dep):
        x_copy(m).start()
    for m in range(1, n_dep):
        x_wait(m).wait()
    total = RX[0].astype(F32)
    for m in range(1, n_dep):
        total = total + RX[m].astype(F32)
    FS[core] = total

    def f_copy(slot):
        return pltpu.make_async_remote_copy(
            src_ref=FS.at[core],
            dst_ref=FS.at[slot],
            send_sem=f_send,
            recv_sem=f_recv,
            device_id=partner,
            device_id_type=MESH,
        )

    f_copy(core).start()
    f_copy(1 - core).wait()

    half = rows // 2
    for t in range(9):
        got = FS[0, t, pl.ds(pl.multiple_of(yl * half, half), half), :]
        g2_out[3 * t] = got[:, :64]
        g2_out[3 * t + 1] = got[:, 64:]
    taps = [(a, b) for a in range(3) for b in (0, 1)] + [(0, 2), (1, 2), (2, 2)]
    for n, (a, b) in enumerate(taps):
        got = FS[1, n // 2, pl.ds(pl.multiple_of(yl * half, half), half), :]
        g2_out[9 * a + 3 * b + 2] = got[:, (n % 2) * 64 : (n % 2) * 64 + 64]
    own = half // 2
    for block in range(7):
        both = FS[1, 5 + block // 2, (block % 2) * half : (block % 2) * half + half, :]
        got = jnp.where(yl == 0, both[:own], both[own:])
        for n in range(4 if block < 6 else 3):
            lanes = got[:, n * 32 : n * 32 + 32]
            if block < 6:
                g1_out[3 * (4 * (block % 2) + n) + block // 2] = lanes
            else:
                g1_out[24 + n] = lanes

    halo(v_copy, 1, "wait_send")
    halo(b_copy, 1, "wait_send")


def per_device(sizes, volume, kernel_first, kernel_second, cotangent):
    n_z, n_y, n_dep, n_hgt = sizes
    rows = 128 // n_z
    vmem = pl.BlockSpec(memory_space=pltpu.VMEM)
    dma = pltpu.SemaphoreType.DMA
    features, grad_first, grad_second = pl.pallas_call(
        functools.partial(kernel, sizes),
        out_shape=(
            jax.ShapeDtypeStruct((128, 2, 8, W), BF),
            jax.ShapeDtypeStruct((27, rows // 4, 32), F32),
            jax.ShapeDtypeStruct((27, rows // 2, 64), F32),
        ),
        in_specs=[vmem] * 4,
        out_specs=(vmem, vmem, vmem),
        scratch_shapes=[
            pltpu.VMEM((6, 12, 32, W), BF),
            pltpu.VMEM((2, 12, 128, W), BF),
            pltpu.VMEM((1024, W), F32),
            pltpu.VMEM((192, 288), BF),
            pltpu.VMEM((384, 576), BF),
            pltpu.VMEM((576, 384), BF),
            pltpu.VMEM((4, 10, 64, W), BF),
            pltpu.VMEM((2, 10, 64, W), F32),
            pltpu.VMEM((2, 8, 64, W), BF),
            pltpu.VMEM((2, 2, 64, W), BF),
            pltpu.VMEM((4, 64, W), BF),
            pltpu.VMEM((4, 10, 64, W), BF),
            pltpu.VMEM((4, 10, 192, W), BF),
            pltpu.VMEM((2, 10, 64, W), F32),
            pltpu.VMEM((16, 192, W), BF),
            pltpu.VMEM((2, n_z, 9, rows, W), F32),
            pltpu.VMEM((2, n_z, 9, rows, W), BF),
            pltpu.VMEM((n_z, 9, rows, W), BF),
            pltpu.VMEM((n_z, 9, rows, W), BF),
            pltpu.VMEM((n_z, 9, rows, W), BF),
            pltpu.VMEM((n_y, 9, rows, W), BF),
            pltpu.VMEM((n_dep, 9, rows, W), BF),
            pltpu.VMEM((2, 9, rows, W), F32),
            pltpu.VMEM((2, 1024, W), F32),
            dma((8,)),
            dma((8,)),
            dma((8,)),
            dma((8,)),
            dma,
            dma,
            dma((n_z,)),
            dma((n_z,)),
            dma((n_y,)),
            dma((n_y,)),
            dma((n_dep,)),
            dma((n_dep,)),
            dma,
            dma,
        ],
        compiler_params=pltpu.CompilerParams(
            collective_id=0, has_side_effects=True, vmem_limit_bytes=50 * 1024 * 1024
        ),
    )(
        volume[0],
        kernel_first.swapaxes(1, 2),
        kernel_second.swapaxes(1, 2),
        cotangent[0],
    )
    return features[None], grad_first, grad_second


def solution(mesh):
    placed = (P("dp", None, "dep", "hgt", None), P(), P(), P("dp", None, "dep", "hgt", None))
    shape = mesh.shape
    sizes = (shape["dp"] // 2, shape["hgt"] // 2 * 2, shape["dep"], shape["hgt"])
    return jax.shard_map(
        functools.partial(per_device, sizes),
        mesh=mesh,
        in_specs=placed,
        out_specs=(P("dp", None, "dep", "hgt", None), P(None, "dp", None), P(None, "dp", None)),
        check_vma=False,
    )
```

```python
import functools

import jax
import jax.numpy as jnp
from jax import lax
from jax.experimental import pallas as pl
from jax.experimental.pallas import tpu as pltpu
from jax.sharding import PartitionSpec as P

MESH = pl.DeviceIdType.MESH
BF = jnp.bfloat16
F32 = jnp.float32
W = 128
DIRS = [(a, b) for a in (-1, 0, 1) for b in (-1, 0, 1) if (a, b) != (0, 0)]
NT = (((1,), (1,)), ((), ()))


def dot(a, b):
    return jnp.dot(a, b, preferred_element_type=F32)


def shifted(x, by):
    if by == 0:
        return x
    lane = lax.broadcasted_iota(jnp.int32, x.shape, 1)
    keep = lane >= by if by > 0 else lane < W + by
    return jnp.where(keep, pltpu.roll(x, by % W, 1), 0.0)


def pair(ref, d, h, rows):
    halves = [ref[d + e, pl.ds(h, 3)].reshape(rows, W) for e in (0, 1)]
    return jnp.concatenate(halves, axis=1)


def kernel(
    sizes,
    vol_hbm,
    k1t_hbm,
    k2t_hbm,
    cot_hbm,
    feat,
    g1_out,
    g2_out,
    vol,
    k1t,
    k2t,
    cot,
    V,
    C,
    tmp,
    W1,
    W2,
    WB,
    BS,
    BO,
    RBX,
    RBH,
    RBD,
    H,
    H3,
    DS,
    D3,
    GA,
    GA16,
    RCA,
    YSA,
    RYA,
    TA,
    ZSA,
    RZA,
    RXA,
    FA,
    GB,
    GB16,
    RCB,
    ZSB,
    RZB,
    YSB,
    RYB,
    RXB,
    FB,
    FO,
    in_sem,
    v_send,
    v_recv,
    b_send,
    b_recv,
    ca_send,
    ca_recv,
    ya_send,
    ya_recv,
    za_send,
    za_recv,
    xa_send,
    xa_recv,
    fa_send,
    fa_recv,
    cb_send,
    cb_recv,
    zb_send,
    zb_recv,
    yb_send,
    yb_recv,
    xb_send,
    xb_recv,
    fb_send,
    fb_recv,
):
    n_z, n_y, n_dep, n_hgt = sizes
    rows = 128 // n_z
    dp, dep, hgt = (lax.axis_index(name) for name in ("dp", "dep", "hgt"))
    z, yl = dp // 2, dp % 2
    yh, core = hgt // 2, hgt % 2
    y = yh * 2 + yl

    def there(direction, sign):
        d, h = dep + sign * direction[0], hgt + sign * direction[1]
        return (d >= 0) & (d < n_dep) & (h >= 0) & (h < n_hgt)

    def z_peer(m):
        return (((z + m) % n_z) * 2 + yl, dep, hgt)

    def y_peer(m):
        other = (y + m) % n_y
        return (z * 2 + other % 2, dep, (other // 2) * 2 + core)

    def x_peer(m):
        return (dp, (dep + m) % n_dep, hgt)

    def y_far(m):
        other = (y + m) % n_y
        return (z * 2 + other % 2, dep, (other // 2) * 2 + 1 - core)

    partner = (dp, dep, hgt + 1 - 2 * core)

    loads = [
        pltpu.make_async_copy(src, dst, in_sem.at[n])
        for n, (src, dst) in enumerate(
            ((vol_hbm, vol), (cot_hbm, cot), (k2t_hbm, k2t), (k1t_hbm, k1t))
        )
    ]
    for load in loads:
        load.start()

    V[...] = jnp.zeros_like(V)
    RBX[...] = jnp.zeros_like(RBX)
    RBH[...] = jnp.zeros_like(RBH)
    RBD[...] = jnp.zeros_like(RBD)

    barrier = pltpu.get_barrier_semaphore()
    for direction in DIRS:

        @pl.when(there(direction, 1))
        def _():
            pl.semaphore_signal(
                barrier,
                inc=1,
                device_id=(dp, dep + direction[0], hgt + direction[1]),
                device_id_type=MESH,
            )

    peers = [partner]
    peers += [z_peer(m) for m in range(1, n_z)]
    peers += [y_peer(m) for m in range(1, n_y)]
    peers += [y_far(m) for m in range(1, n_y)]
    peers += [x_peer(m) for m in range(1, n_dep)]
    for peer in peers:
        pl.semaphore_signal(barrier, inc=1, device_id=peer, device_id_type=MESH)

    loads[0].wait()
    for d in (0, 1):
        tmp[0:256, :] = vol[:, d].astype(F32).reshape(256, W)
        for h in range(8):
            V[2 + d, 2 + h] = tmp[pl.ds(h, 32, stride=8), :].astype(BF)

    loads[1].wait()
    for d in (0, 1):
        for h in (0, 1, 10, 11):
            C[d, h] = jnp.zeros((128, W), BF)
        tmp[...] = cot[:, d].astype(F32).reshape(1024, W)

        @pl.loop(0, 8, unroll=4)
        def _(h):
            C[d, 2 + h] = tmp[pl.ds(h, 128, stride=8), :].astype(BF)

    loads[2].wait()
    for a in range(3):
        for b in range(3):
            for c in range(3):
                WB[a * 192 + c * 64 : a * 192 + c * 64 + 64, (2 - b) * 128 : (3 - b) * 128] = k2t[
                    9 * a + 3 * b + c
                ]

    span_d = 1 + (dep > 0).astype(jnp.int32) + (dep < n_dep - 1).astype(jnp.int32)
    span_h = 1 + (hgt > 0).astype(jnp.int32) + (hgt < n_hgt - 1).astype(jnp.int32)
    pl.semaphore_wait(barrier, span_d * span_h - 1 + len(peers))

    def v_copy(k):
        a, b = DIRS[k]
        to_d = {0: (2, 4), 1: (0, 2), -1: (4, 6)}[a]
        from_h, to_h = {0: ((2, 10), (2, 10)), 1: ((8, 10), (0, 2)), -1: ((2, 4), (10, 12))}[b]
        return pltpu.make_async_remote_copy(
            src_ref=V.at[2:4, from_h[0] : from_h[1]],
            dst_ref=V.at[to_d[0] : to_d[1], to_h[0] : to_h[1]],
            send_sem=v_send.at[k],
            recv_sem=v_recv.at[k],
            device_id=(dp, dep + a, hgt + b),
            device_id_type=MESH,
        )

    def b_copy(k):
        a, b = DIRS[k]
        d = {-1: 0, 1: 3}.get(a)
        h = {-1: 0, 1: 9}.get(b)
        if a == 0:
            src, dst = BS.at[1:3, h], RBH.at[(b + 1) // 2]
        elif b == 0:
            src, dst = BS.at[d, 1:9], RBX.at[(a + 1) // 2]
        else:
            src, dst = BS.at[d, h], RBD.at[(a + 1) + (b + 1) // 2]
        return pltpu.make_async_remote_copy(
            src_ref=src,
            dst_ref=dst,
            send_sem=b_send.at[k],
            recv_sem=b_recv.at[k],
            device_id=(dp, dep + a, hgt + b),
            device_id_type=MESH,
        )

    def halo(copy, sign, what):
        for k, direction in enumerate(DIRS):

            @pl.when(there(direction, sign))
            def _():
                getattr(copy(k), what)()

    halo(v_copy, 1, "start")

    @pl.loop(0, 10, unroll=5)
    def _(h):
        t = dot(WB[...], pair(C, 0, h, 384))
        sums = []
        for a in range(3):
            halves = []
            for e in (0, 1):
                parts = [
                    shifted(t[a * 192 + c * 64 : a * 192 + c * 64 + 64, e * W : e * W + W], c - 1)
                    for c in range(3)
                ]
                halves.append(parts[0] + parts[1] + parts[2])
            sums.append(halves)
        inner = [sums[0][1] + sums[1][0], sums[1][1] + sums[2][0]]
        BS[0, h] = sums[0][0].astype(BF)
        BS[3, h] = sums[2][1].astype(BF)
        for d in (0, 1):
            BS[1 + d, h] = inner[d].astype(BF)
            BO[d, h] = inner[d]

    halo(b_copy, 1, "start")

    loads[3].wait()
    for c in range(3):
        stack = [k1t[3 * t + c].astype(F32) for t in range(9)]
        W1[c * 64 : c * 64 + 64, :] = jnp.concatenate(stack, axis=0).T.astype(BF)

    halo(v_copy, -1, "wait_recv")

    @pl.loop(0, 10, unroll=5)
    def _(h):
        ok_h = ((h > 0) | (hgt > 0)) & ((h < 9) | (hgt < n_hgt - 1))
        for d in (0, 2):
            x = jnp.concatenate([pair(V, d + a, h, 96) for a in range(3)], axis=0)
            t = dot(W1[...], x)
            for e in (0, 1):
                part = [t[c * 64 : c * 64 + 64, e * W : e * W + W] for c in range(3)]
                pre = shifted(part[0], 1) + part[1] + shifted(part[2], -1)
                sigma = 0.5 * jnp.tanh(0.5 * pre) + 0.5
                ok = ok_h
                if d + e == 0:
                    ok = ok & (dep > 0)
                elif d + e == 3:
                    ok = ok & (dep < n_dep - 1)
                hid = pre * sigma * ok.astype(F32)
                H[d + e, h] = hid.astype(BF)
                for c in range(3):
                    H3[d + e, h, c * 64 : c * 64 + 64] = shifted(hid, 1 - c).astype(BF)
                if d + e in (1, 2):
                    DS[d + e - 1, h] = sigma * (1.0 + pre * (1.0 - sigma))

    def keep(owner, unit, value):
        if unit < 4:
            GA[owner, unit] = value
            GA16[owner, unit] = value.astype(BF)
        else:
            value = value.reshape(n_z, rows, W)
            GB[owner, :, unit - 4] = value
            GB16[owner, :, unit - 4] = value.astype(BF)

    upstream = [C[d, 2 + h] for h in range(8) for d in (0, 1)]
    upstream = jnp.concatenate(upstream, axis=1)
    lasts = {}
    for a in range(3):
        for b in range(3):
            field = [H3[d + a, h + b] for h in range(8) for d in (0, 1)]
            part = lax.dot_general(
                upstream, jnp.concatenate(field, axis=1), NT, preferred_element_type=F32
            )
            keep(0, 3 * a + b, part[:, :128])
            lasts[a, b] = part[:, 128:192]
        keep(1, a, jnp.concatenate([lasts[a, 0], lasts[a, 1]], axis=1))
    keep(1, 3, jnp.concatenate([lasts[0, 2], lasts[1, 2]], axis=1))
    keep(1, 4, jnp.concatenate([lasts[2, 2], jnp.zeros((128, 64), F32)], axis=1))

    def remote(src, dst, send, recv, peer):
        return pltpu.make_async_remote_copy(
            src_ref=src,
            dst_ref=dst,
            send_sem=send,
            recv_sem=recv,
            device_id=peer,
            device_id_type=MESH,
        )

    ca = remote(GA16.at[1 - core], RCA, ca_send, ca_recv, partner)
    cb = remote(GB16.at[1 - core], RCB, cb_send, cb_recv, partner)
    ya = [remote(YSA.at[(y + m) % n_y], RYA.at[m], ya_send.at[m], ya_recv.at[m], y_peer(m)) for m in range(1, n_y)]
    za = [remote(ZSA.at[(z + m) % n_z], RZA.at[m], za_send.at[m], za_recv.at[m], z_peer(m)) for m in range(1, n_z)]
    zb = [remote(ZSB.at[(z + m) % n_z], RZB.at[m], zb_send.at[m], zb_recv.at[m], z_peer(m)) for m in range(1, n_z)]

    def x_copies(buf, send, recv, arriving):
        return [
            remote(
                buf.at[dep],
                buf.at[(dep + n_dep - m) % n_dep if arriving else dep],
                send.at[m],
                recv.at[m],
                x_peer(m),
            )
            for m in range(1, n_dep)
        ]

    def yb_copies(arriving):
        return [
            remote(
                YSB.at[(y + m) % 2],
                RYB.at[(y + n_y - m) % n_y if arriving else y],
                yb_send.at[m],
                yb_recv.at[m],
                y_peer(m),
            )
            for m in range(1, n_y)
        ]

    def fa_copies(arriving):
        copies = []
        for m in range(1, n_y):
            for far in (0, 1):
                from_core = (1 - core if far else core) if arriving else core
                from_y = (y + n_y - m) % n_y if arriving else y
                to_yl = yl if arriving else (y + m) % 2
                copies.append(
                    remote(
                        FA.at[core, y, (y + m) % 2],
                        FA.at[from_core, from_y, to_yl],
                        fa_send.at[2 * m + far],
                        fa_recv.at[2 * m + far],
                        y_far(m) if far else y_peer(m),
                    )
                )
        copies.append(
            remote(
                FA.at[core, y, yl],
                FA.at[1 - core if arriving else core, y, yl],
                fa_send.at[0],
                fa_recv.at[0],
                partner,
            )
        )
        return copies

    def start(copies):
        for copy in copies:
            copy.start()

    def wait(copies):
        for copy in copies:
            copy.wait()

    def z_first():
        cb.wait_recv()

        @pl.loop(0, n_z, unroll=4)
        def _(j):
            ZSB[j] = (GB[core, j] + RCB[j].astype(F32)).astype(BF)

        start(zb)

    ca.start()

    @pl.when(core == 1)
    def _():
        cb.start()

    halo(b_copy, -1, "wait_recv")

    for d, a in ((0, 1), (1, -1)):
        for h, b in ((0, 1), (7, -1)):
            BO[d, 1 + h] += RBH[(b + 1) // 2, d].astype(F32) + RBD[(a + 1) + (b + 1) // 2].astype(F32)

    @pl.loop(0, 8, unroll=4)
    def _(h):
        for d, a in ((0, 1), (1, -1)):
            back = BO[d, 1 + h] + RBX[(a + 1) // 2, h].astype(F32)
            delta = back * DS[d, 1 + h]
            for c in range(3):
                D3[2 * h + d, c * 64 : c * 64 + 64] = shifted(delta, c - 1).astype(BF)

    ca.wait()
    for j in range(n_y):
        for u in range(4 // n_y):
            unit = j * (4 // n_y) + u
            YSA[j, u] = (GA[core, unit] + RCA[unit].astype(F32)).astype(BF)
    start(ya)

    @pl.when(core == 0)
    def _():
        z_first()

    upstream = jnp.concatenate([D3[r] for r in range(16)], axis=1)
    field = [
        jnp.concatenate(
            [V[2 + d + a - 1, 2 + h - 1 : 2 + h + 2].reshape(96, W) for a in range(3)], axis=0
        )
        for h in range(8)
        for d in (0, 1)
    ]
    part = lax.dot_general(
        upstream, jnp.concatenate(field, axis=1), NT, preferred_element_type=F32
    )
    blocks = [part[c * 64 : c * 64 + 64, j * W : j * W + W] for c in range(3) for j in (0, 1)]
    ends = [part[c * 64 : c * 64 + 64, 256:288] for c in range(3)]
    blocks.append(jnp.concatenate(ends + [jnp.zeros((64, 32), F32)], axis=1))
    blocks.append(jnp.zeros((64, W), F32))
    for m in range(4):
        two = [blocks[2 * m + e].reshape(n_z, rows // 2, W) for e in (0, 1)]
        part = [two[e][:, f * (rows // 4) : (f + 1) * (rows // 4)] for f in (0, 1) for e in (0, 1)]
        value = jnp.concatenate(part, axis=1)
        GB[1, :, 1 + m] = value
        GB16[1, :, 1 + m] = value.astype(BF)

    @pl.when(core == 0)
    def _():
        cb.start()

    for c in range(3):
        stack = [k2t[3 * t + c].astype(F32) for t in range(9)]
        W2[c * 128 : c * 128 + 128, :] = jnp.concatenate(stack, axis=0).T.astype(BF)

    @pl.when(core == 1)
    def _():
        z_first()

    cb.wait_send()

    def features(h):
        x = jnp.concatenate([pair(H, a, h, 192) for a in range(3)], axis=0)
        t = dot(W2[...], x)
        for d in (0, 1):
            part = [t[c * 128 : c * 128 + 128, d * W : d * W + W] for c in range(3)]
            total = shifted(part[0], 1) + part[1] + shifted(part[2], -1)
            FO[d, pl.ds(h, 128, stride=8), :] = total

    pl.loop(0, 4, unroll=4)(features)

    wait(ya)
    per = 4 // n_y
    for u in range(per):
        total = GA[core, y * per + u] + RCA[y * per + u].astype(F32)
        for m in range(1, n_y):
            total = total + RYA[m, u].astype(F32)
        total = total.reshape(n_z, rows, W)
        TA[:, u] = total
        ZSA[:, u] = total.astype(BF)
    start(za)

    pl.loop(4, 8, unroll=4)(features)
    for d in (0, 1):
        feat[:, d] = FO[d].reshape(128, 8, W).astype(BF)

    half = rows // 2
    wait(zb)
    total = GB[core, z] + RCB[z].astype(F32)
    for m in range(1, n_z):
        total = total + RZB[m].astype(F32)
    for e in (0, 1):
        YSB[e] = total[:, e * half : (e + 1) * half].astype(BF)
    RYB[y] = YSB[yl]
    start(yb_copies(False))

    wait(za)
    total = TA[z]
    for m in range(1, n_z):
        total = total + RZA[m].astype(F32)
    RXA[dep] = total.astype(BF)
    start(x_copies(RXA, xa_send, xa_recv, False))

    wait(yb_copies(True))
    total = RYB[0].astype(F32)
    for m in range(1, n_y):
        total = total + RYB[m].astype(F32)
    RXB[dep] = total.astype(BF)
    start(x_copies(RXB, xb_send, xb_recv, False))

    wait(x_copies(RXA, xa_send, xa_recv, True))
    total = RXA[0].astype(F32)
    for m in range(1, n_dep):
        total = total + RXA[m].astype(F32)
    for e in (0, 1):
        FA[core, y, e] = total[:, e * half : (e + 1) * half]
    start(fa_copies(False))

    wait(x_copies(RXB, xb_send, xb_recv, True))
    total = RXB[0].astype(F32)
    for m in range(1, n_dep):
        total = total + RXB[m].astype(F32)
    FB[core] = total
    remote(FB.at[core], FB.at[core], fb_send, fb_recv, partner).start()
    wait(fa_copies(True))
    remote(FB.at[core], FB.at[1 - core], fb_send, fb_recv, partner).wait()

    def unit_of(owner, unit):
        if unit < 4:
            return FA[owner, unit // per, yl, unit % per]
        return FB[owner, unit - 4]

    for t in range(9):
        got = unit_of(0, t)
        g2_out[3 * t] = got[:, :64]
        g2_out[3 * t + 1] = got[:, 64:]
    taps = [(a, b) for a in range(3) for b in (0, 1)] + [(0, 2), (1, 2), (2, 2)]
    for n, (a, b) in enumerate(taps):
        got = unit_of(1, n // 2)
        g2_out[9 * a + 3 * b + 2] = got[:, (n % 2) * 64 : (n % 2) * 64 + 64]
    own = half // 2
    for block in range(7):
        got = FB[1, 1 + block // 2, (block % 2) * own : (block % 2) * own + own, :]
        for n in range(4 if block < 6 else 3):
            lanes = got[:, n * 32 : n * 32 + 32]
            if block < 6:
                g1_out[3 * (4 * (block % 2) + n) + block // 2] = lanes
            else:
                g1_out[24 + n] = lanes

    halo(v_copy, 1, "wait_send")
    halo(b_copy, 1, "wait_send")


def per_device(sizes, volume, kernel_first, kernel_second, cotangent):
    n_z, n_y, n_dep, n_hgt = sizes
    rows, per = 128 // n_z, 4 // n_y
    vmem = pl.BlockSpec(memory_space=pltpu.VMEM)
    dma = pltpu.SemaphoreType.DMA
    features, grad_first, grad_second = pl.pallas_call(
        functools.partial(kernel, sizes),
        out_shape=(
            jax.ShapeDtypeStruct((128, 2, 8, W), BF),
            jax.ShapeDtypeStruct((27, rows // 4, 32), F32),
            jax.ShapeDtypeStruct((27, rows // 2, 64), F32),
        ),
        in_specs=[pl.BlockSpec(memory_space=pltpu.HBM)] * 4,
        out_specs=(vmem, vmem, vmem),
        scratch_shapes=[
            pltpu.VMEM((32, 2, 8, W), BF),
            pltpu.VMEM((27, 32, 64), BF),
            pltpu.VMEM((27, 64, 128), BF),
            pltpu.VMEM((128, 2, 8, W), BF),
            pltpu.VMEM((6, 12, 32, W), BF),
            pltpu.VMEM((2, 12, 128, W), BF),
            pltpu.VMEM((1024, W), F32),
            pltpu.VMEM((192, 288), BF),
            pltpu.VMEM((384, 576), BF),
            pltpu.VMEM((576, 384), BF),
            pltpu.VMEM((4, 10, 64, W), BF),
            pltpu.VMEM((2, 10, 64, W), F32),
            pltpu.VMEM((2, 8, 64, W), BF),
            pltpu.VMEM((2, 2, 64, W), BF),
            pltpu.VMEM((4, 64, W), BF),
            pltpu.VMEM((4, 10, 64, W), BF),
            pltpu.VMEM((4, 10, 192, W), BF),
            pltpu.VMEM((2, 10, 64, W), F32),
            pltpu.VMEM((16, 192, W), BF),
            pltpu.VMEM((2, 4, 128, W), F32),
            pltpu.VMEM((2, 4, 128, W), BF),
            pltpu.VMEM((4, 128, W), BF),
            pltpu.VMEM((n_y, per, 128, W), BF),
            pltpu.VMEM((n_y, per, 128, W), BF),
            pltpu.VMEM((n_z, per, rows, W), F32),
            pltpu.VMEM((n_z, per, rows, W), BF),
            pltpu.VMEM((n_z, per, rows, W), BF),
            pltpu.VMEM((n_dep, per, rows, W), BF),
            pltpu.VMEM((2, n_y, 2, per, rows // 2, W), F32),
            pltpu.VMEM((2, n_z, 5, rows, W), F32),
            pltpu.VMEM((2, n_z, 5, rows, W), BF),
            pltpu.VMEM((n_z, 5, rows, W), BF),
            pltpu.VMEM((n_z, 5, rows, W), BF),
            pltpu.VMEM((n_z, 5, rows, W), BF),
            pltpu.VMEM((2, 5, rows // 2, W), BF),
            pltpu.VMEM((n_y, 5, rows // 2, W), BF),
            pltpu.VMEM((n_dep, 5, rows // 2, W), BF),
            pltpu.VMEM((2, 5, rows // 2, W), F32),
            pltpu.VMEM((2, 1024, W), F32),
            dma((4,)),
            dma((8,)),
            dma((8,)),
            dma((8,)),
            dma((8,)),
            dma,
            dma,
            dma((n_y,)),
            dma((n_y,)),
            dma((n_z,)),
            dma((n_z,)),
            dma((n_dep,)),
            dma((n_dep,)),
            dma((2 * n_y,)),
            dma((2 * n_y,)),
            dma,
            dma,
            dma((n_z,)),
            dma((n_z,)),
            dma((n_y,)),
            dma((n_y,)),
            dma((n_dep,)),
            dma((n_dep,)),
            dma,
            dma,
        ],
        compiler_params=pltpu.CompilerParams(
            collective_id=0, has_side_effects=True, vmem_limit_bytes=40 * 1024 * 1024
        ),
    )(
        volume[0],
        kernel_first.swapaxes(1, 2),
        kernel_second.swapaxes(1, 2),
        cotangent[0],
    )
    return features[None], grad_first, grad_second


def solution(mesh):
    placed = (P("dp", None, "dep", "hgt", None), P(), P(), P("dp", None, "dep", "hgt", None))
    shape = mesh.shape
    sizes = (shape["dp"] // 2, shape["hgt"] // 2 * 2, shape["dep"], shape["hgt"])
    return jax.shard_map(
        functools.partial(per_device, sizes),
        mesh=mesh,
        in_specs=placed,
        out_specs=(P("dp", None, "dep", "hgt", None), P(None, "dp", None), P(None, "dp", None)),
        check_vma=False,
    )
```

```python
import functools

import jax
import jax.numpy as jnp
from jax import lax
from jax.experimental import pallas as pl
from jax.experimental.pallas import tpu as pltpu
from jax.sharding import PartitionSpec as P

MESH = pl.DeviceIdType.MESH
BF = jnp.bfloat16
F32 = jnp.float32
W = 128
DIRS = [(a, b) for a in (-1, 0, 1) for b in (-1, 0, 1) if (a, b) != (0, 0)]
NT = (((1,), (1,)), ((), ()))


def dot(a, b):
    return jnp.dot(a, b, preferred_element_type=F32)


def shifted(x, by):
    if by == 0:
        return x
    lane = lax.broadcasted_iota(jnp.int32, x.shape, 1)
    keep = lane >= by if by > 0 else lane < W + by
    return jnp.where(keep, pltpu.roll(x, by % W, 1), 0.0)


def pair(ref, d, h, rows):
    halves = [ref[d + e, pl.ds(h, 3)].reshape(rows, W) for e in (0, 1)]
    return jnp.concatenate(halves, axis=1)


def kernel(
    sizes,
    vol_hbm,
    k1t_hbm,
    k2t_hbm,
    cot_hbm,
    feat,
    g1_out,
    g2_out,
    vol,
    k1t,
    k2t,
    cot,
    V,
    C,
    tmp,
    W1,
    W2,
    WB,
    BS,
    BO,
    RBX,
    RBH,
    RBD,
    H,
    H3,
    DS,
    D3,
    GA,
    GA16,
    RCA,
    YSA,
    RYA,
    TA,
    ZSA,
    RZA,
    RXA,
    FA,
    GB,
    GB16,
    RCB,
    ZSB,
    RZB,
    YSB,
    RYB,
    RXB,
    FB,
    FO,
    in_sem,
    v_send,
    v_recv,
    b_send,
    b_recv,
    ca_send,
    ca_recv,
    ya_send,
    ya_recv,
    za_send,
    za_recv,
    xa_send,
    xa_recv,
    fa_send,
    fa_recv,
    cb_send,
    cb_recv,
    zb_send,
    zb_recv,
    yb_send,
    yb_recv,
    xb_send,
    xb_recv,
):
    n_z, n_y, n_dep, n_hgt = sizes
    rows = 128 // n_z
    dp, dep, hgt = (lax.axis_index(name) for name in ("dp", "dep", "hgt"))
    z, yl = dp // 2, dp % 2
    yh, core = hgt // 2, hgt % 2
    y = yh * 2 + yl

    def there(direction, sign):
        d, h = dep + sign * direction[0], hgt + sign * direction[1]
        return (d >= 0) & (d < n_dep) & (h >= 0) & (h < n_hgt)

    def z_peer(m):
        return (((z + m) % n_z) * 2 + yl, dep, hgt)

    def y_peer(m):
        other = (y + m) % n_y
        return (z * 2 + other % 2, dep, (other // 2) * 2 + core)

    def x_peer(m):
        return (dp, (dep + m) % n_dep, hgt)

    def y_far(m):
        other = (y + m) % n_y
        return (z * 2 + other % 2, dep, (other // 2) * 2 + 1 - core)

    def x_far(m):
        return (dp, (dep + m) % n_dep, hgt + 1 - 2 * core)

    partner = (dp, dep, hgt + 1 - 2 * core)

    loads = [
        pltpu.make_async_copy(src, dst, in_sem.at[n])
        for n, (src, dst) in enumerate(
            ((vol_hbm, vol), (cot_hbm, cot), (k2t_hbm, k2t), (k1t_hbm, k1t))
        )
    ]
    for load in loads:
        load.start()

    barrier = pltpu.get_barrier_semaphore()
    for direction in DIRS:

        @pl.when(there(direction, 1))
        def _():
            pl.semaphore_signal(
                barrier,
                inc=1,
                device_id=(dp, dep + direction[0], hgt + direction[1]),
                device_id_type=MESH,
            )

    peers = [partner]
    peers += [z_peer(m) for m in range(1, n_z)]
    peers += [y_peer(m) for m in range(1, n_y)]
    peers += [y_far(m) for m in range(1, n_y)]
    peers += [x_peer(m) for m in range(1, n_dep)]
    peers += [x_far(m) for m in range(1, n_dep)]
    for peer in peers:
        pl.semaphore_signal(barrier, inc=1, device_id=peer, device_id_type=MESH)

    for k, (a, b) in enumerate(DIRS):
        rows_d = {0: (2, 4), 1: (0, 2), -1: (4, 6)}[a]
        rows_h = {0: (2, 10), 1: (0, 2), -1: (10, 12)}[b]

        @pl.when(jnp.logical_not(there((a, b), -1)))
        def _():
            block = V.at[rows_d[0] : rows_d[1], rows_h[0] : rows_h[1]]
            block[...] = jnp.zeros(block.shape, BF)
            if a == 0:
                part = RBH.at[(b + 1) // 2]
            elif b == 0:
                part = RBX.at[(a + 1) // 2]
            else:
                part = RBD.at[(a + 1) + (b + 1) // 2]
            part[...] = jnp.zeros(part.shape, BF)

    loads[0].wait()
    for d in (0, 1):
        tmp[0:256, :] = vol[:, d].astype(F32).reshape(256, W)
        for h in range(8):
            V[2 + d, 2 + h] = tmp[pl.ds(h, 32, stride=8), :].astype(BF)

    loads[1].wait()
    for d in (0, 1):
        for h in (0, 1, 10, 11):
            C[d, h] = jnp.zeros((128, W), BF)
        tmp[...] = cot[:, d].astype(F32).reshape(1024, W)

        @pl.loop(0, 8, unroll=4)
        def _(h):
            C[d, 2 + h] = tmp[pl.ds(h, 128, stride=8), :].astype(BF)

    loads[2].wait()
    for a in range(3):
        for b in range(3):
            for c in range(3):
                WB[a * 192 + c * 64 : a * 192 + c * 64 + 64, (2 - b) * 128 : (3 - b) * 128] = k2t[
                    9 * a + 3 * b + c
                ]

    span_d = 1 + (dep > 0).astype(jnp.int32) + (dep < n_dep - 1).astype(jnp.int32)
    span_h = 1 + (hgt > 0).astype(jnp.int32) + (hgt < n_hgt - 1).astype(jnp.int32)
    pl.semaphore_wait(barrier, span_d * span_h - 1 + len(peers))

    def v_copy(k, far):
        a, b = DIRS[k]
        from_h, to_h = {0: ((2, 10), (2, 10)), 1: ((8, 10), (0, 2)), -1: ((2, 4), (10, 12))}[b]
        if a == 0:
            src, dst = V.at[2:4, from_h[0] : from_h[1]], V.at[2:4, to_h[0] : to_h[1]]
        else:
            plane = {(1, 0): (3, 1), (1, 1): (2, 0), (-1, 0): (2, 4), (-1, 1): (3, 5)}[a, far]
            src, dst = V.at[plane[0], from_h[0] : from_h[1]], V.at[plane[1], to_h[0] : to_h[1]]
        return pltpu.make_async_remote_copy(
            src_ref=src,
            dst_ref=dst,
            send_sem=v_send.at[far, k],
            recv_sem=v_recv.at[far, k],
            device_id=(dp, dep + a, hgt + b),
            device_id_type=MESH,
        )

    def near(k):
        return v_copy(k, 0)

    def far(k):
        return v_copy(k, 1) if DIRS[k][0] != 0 else None

    def b_copy(k):
        a, b = DIRS[k]
        d = {-1: 0, 1: 3}.get(a)
        h = {-1: 0, 1: 9}.get(b)
        if a == 0:
            src, dst = BS.at[1:3, h], RBH.at[(b + 1) // 2]
        elif b == 0:
            src, dst = BS.at[d, 1:9], RBX.at[(a + 1) // 2]
        else:
            src, dst = BS.at[d, h], RBD.at[(a + 1) + (b + 1) // 2]
        return pltpu.make_async_remote_copy(
            src_ref=src,
            dst_ref=dst,
            send_sem=b_send.at[k],
            recv_sem=b_recv.at[k],
            device_id=(dp, dep + a, hgt + b),
            device_id_type=MESH,
        )

    def halo(copy, sign, what):
        for k, direction in enumerate(DIRS):

            @pl.when(there(direction, sign))
            def _():
                one = copy(k)
                if one is not None:
                    getattr(one, what)()

    halo(near, 1, "start")
    halo(far, 1, "start")

    @pl.loop(0, 10, unroll=5)
    def _(h):
        t = dot(WB[...], pair(C, 0, h, 384))
        sums = []
        for a in range(3):
            halves = []
            for e in (0, 1):
                parts = [
                    shifted(t[a * 192 + c * 64 : a * 192 + c * 64 + 64, e * W : e * W + W], c - 1)
                    for c in range(3)
                ]
                halves.append(parts[0] + parts[1] + parts[2])
            sums.append(halves)
        inner = [sums[0][1] + sums[1][0], sums[1][1] + sums[2][0]]
        BS[0, h] = sums[0][0].astype(BF)
        BS[3, h] = sums[2][1].astype(BF)
        for d in (0, 1):
            BS[1 + d, h] = inner[d].astype(BF)
            BO[d, h] = inner[d]

    halo(b_copy, 1, "start")

    loads[3].wait()
    for c in range(3):
        stack = [k1t[3 * t + c].astype(F32) for t in range(9)]
        W1[c * 64 : c * 64 + 64, :] = jnp.concatenate(stack, axis=0).T.astype(BF)

    halo(near, -1, "wait_recv")

    def hidden(planes):
        def body(h):
            ok_h = ((h > 0) | (hgt > 0)) & ((h < 9) | (hgt < n_hgt - 1))
            x = [
                jnp.concatenate([V[d + a, pl.ds(h, 3)].reshape(96, W) for d in planes], axis=1)
                for a in range(3)
            ]
            t = dot(W1[...], jnp.concatenate(x, axis=0))
            for e, d in enumerate(planes):
                part = [t[c * 64 : c * 64 + 64, e * W : e * W + W] for c in range(3)]
                pre = shifted(part[0], 1) + part[1] + shifted(part[2], -1)
                sigma = 0.5 * jnp.tanh(0.5 * pre) + 0.5
                ok = {0: ok_h & (dep > 0), 3: ok_h & (dep < n_dep - 1)}.get(d, ok_h)
                hid = pre * sigma * ok.astype(F32)
                H[d, h] = hid.astype(BF)
                for c in range(3):
                    H3[d, h, c * 64 : c * 64 + 64] = shifted(hid, 1 - c).astype(BF)
                if d in (1, 2):
                    DS[d - 1, h] = sigma * (1.0 + pre * (1.0 - sigma))

        pl.loop(0, 10, unroll=5)(body)

    def keep(owner, unit, value):
        if unit < 4:
            GA[owner, unit] = value
            GA16[owner, unit] = value.astype(BF)
        else:
            value = value.reshape(n_z, rows, W)
            GB[owner, :, unit - 4] = value
            GB16[owner, :, unit - 4] = value.astype(BF)

    lasts = {}

    def second(a):
        upstream = [C[d, 2 + h] for h in range(8) for d in (0, 1)]
        upstream = jnp.concatenate(upstream, axis=1)
        for b in range(3):
            field = [H3[d + a, h + b] for h in range(8) for d in (0, 1)]
            part = lax.dot_general(
                upstream, jnp.concatenate(field, axis=1), NT, preferred_element_type=F32
            )
            keep(0, 3 * a + b, part[:, :128])
            lasts[a, b] = part[:, 128:192]
        keep(1, a, jnp.concatenate([lasts[a, 0], lasts[a, 1]], axis=1))

    hidden((1, 2))
    second(1)
    halo(far, -1, "wait_recv")
    hidden((0, 3))
    second(0)
    keep(1, 3, jnp.concatenate([lasts[0, 2], lasts[1, 2]], axis=1))
    second(2)
    keep(1, 4, jnp.concatenate([lasts[2, 2], jnp.zeros((128, 64), F32)], axis=1))

    def remote(src, dst, send, recv, peer):
        return pltpu.make_async_remote_copy(
            src_ref=src,
            dst_ref=dst,
            send_sem=send,
            recv_sem=recv,
            device_id=peer,
            device_id_type=MESH,
        )

    ca = remote(GA16.at[1 - core], RCA, ca_send, ca_recv, partner)
    cb = remote(GB16.at[1 - core], RCB, cb_send, cb_recv, partner)
    ya = [remote(YSA.at[(y + m) % n_y], RYA.at[m], ya_send.at[m], ya_recv.at[m], y_peer(m)) for m in range(1, n_y)]
    za = [remote(ZSA.at[(z + m) % n_z], RZA.at[m], za_send.at[m], za_recv.at[m], z_peer(m)) for m in range(1, n_z)]
    zb = [remote(ZSB.at[(z + m) % n_z], RZB.at[m], zb_send.at[m], zb_recv.at[m], z_peer(m)) for m in range(1, n_z)]

    def xa_copies(arriving):
        return [
            remote(
                RXA.at[dep],
                RXA.at[(dep + n_dep - m) % n_dep if arriving else dep],
                xa_send.at[m],
                xa_recv.at[m],
                x_peer(m),
            )
            for m in range(1, n_dep)
        ]

    def xb_copies(arriving):
        copies = []
        for m in range(n_dep):
            for other in (0, 1):
                if m + other > 0:
                    slot = (dep + n_dep - m) % n_dep if arriving else dep
                    half = 1 - core if arriving and other else core
                    copies.append(
                        remote(
                            RXB.at[core, dep],
                            RXB.at[half, slot],
                            xb_send.at[2 * m + other],
                            xb_recv.at[2 * m + other],
                            (x_far if other else x_peer)(m) if m else partner,
                        )
                    )
        return copies

    def yb_copies(arriving):
        return [
            remote(
                YSB.at[(y + m) % 2],
                RYB.at[(y + n_y - m) % n_y if arriving else y],
                yb_send.at[m],
                yb_recv.at[m],
                y_peer(m),
            )
            for m in range(1, n_y)
        ]

    def fa_copies(arriving):
        copies = []
        for m in range(1, n_y):
            for far in (0, 1):
                from_core = (1 - core if far else core) if arriving else core
                from_y = (y + n_y - m) % n_y if arriving else y
                to_yl = yl if arriving else (y + m) % 2
                copies.append(
                    remote(
                        FA.at[core, y, (y + m) % 2],
                        FA.at[from_core, from_y, to_yl],
                        fa_send.at[2 * m + far],
                        fa_recv.at[2 * m + far],
                        y_far(m) if far else y_peer(m),
                    )
                )
        copies.append(
            remote(
                FA.at[core, y, yl],
                FA.at[1 - core if arriving else core, y, yl],
                fa_send.at[0],
                fa_recv.at[0],
                partner,
            )
        )
        return copies

    def start(copies):
        for copy in copies:
            copy.start()

    sent = []

    def wait(copies):
        sent.extend(copies)
        for copy in copies:
            copy.wait_recv()

    def z_first():
        cb.wait_recv()

        @pl.loop(0, n_z, unroll=4)
        def _(j):
            ZSB[j] = (GB[core, j] + RCB[j].astype(F32)).astype(BF)

        start(zb)

    ca.start()

    @pl.when(core == 1)
    def _():
        cb.start()

    halo(b_copy, -1, "wait_recv")

    for d, a in ((0, 1), (1, -1)):
        for h, b in ((0, 1), (7, -1)):
            BO[d, 1 + h] += RBH[(b + 1) // 2, d].astype(F32) + RBD[(a + 1) + (b + 1) // 2].astype(F32)

    @pl.loop(0, 8, unroll=4)
    def _(h):
        for d, a in ((0, 1), (1, -1)):
            back = BO[d, 1 + h] + RBX[(a + 1) // 2, h].astype(F32)
            delta = back * DS[d, 1 + h]
            for c in range(3):
                D3[2 * h + d, c * 64 : c * 64 + 64] = shifted(delta, c - 1).astype(BF)

    ca.wait_recv()
    for j in range(n_y):
        for u in range(4 // n_y):
            unit = j * (4 // n_y) + u
            YSA[j, u] = (GA[core, unit] + RCA[unit].astype(F32)).astype(BF)
    start(ya)

    @pl.when(core == 0)
    def _():
        z_first()

    upstream = jnp.concatenate([D3[r] for r in range(16)], axis=1)
    field = [
        jnp.concatenate(
            [V[2 + d + a - 1, 2 + h - 1 : 2 + h + 2].reshape(96, W) for a in range(3)], axis=0
        )
        for h in range(8)
        for d in (0, 1)
    ]
    part = lax.dot_general(
        upstream, jnp.concatenate(field, axis=1), NT, preferred_element_type=F32
    )
    blocks = [part[c * 64 : c * 64 + 64, j * W : j * W + W] for c in range(3) for j in (0, 1)]
    ends = [part[c * 64 : c * 64 + 64, 256:288] for c in range(3)]
    blocks.append(jnp.concatenate(ends + [jnp.zeros((64, 32), F32)], axis=1))
    blocks.append(jnp.zeros((64, W), F32))
    for m in range(4):
        two = [blocks[2 * m + e].reshape(n_z, rows // 2, W) for e in (0, 1)]
        part = [two[e][:, f * (rows // 4) : (f + 1) * (rows // 4)] for f in (0, 1) for e in (0, 1)]
        value = jnp.concatenate(part, axis=1)
        GB[1, :, 1 + m] = value
        GB16[1, :, 1 + m] = value.astype(BF)

    @pl.when(core == 0)
    def _():
        cb.start()

    for c in range(3):
        stack = [k2t[3 * t + c].astype(F32) for t in range(9)]
        W2[c * 128 : c * 128 + 128, :] = jnp.concatenate(stack, axis=0).T.astype(BF)

    @pl.when(core == 1)
    def _():
        z_first()

    def features(h):
        x = jnp.concatenate([pair(H, a, h, 192) for a in range(3)], axis=0)
        t = dot(W2[...], x)
        for d in (0, 1):
            part = [t[c * 128 : c * 128 + 128, d * W : d * W + W] for c in range(3)]
            total = shifted(part[0], 1) + part[1] + shifted(part[2], -1)
            FO[d, pl.ds(h, 128, stride=8), :] = total

    pl.loop(0, 4, unroll=4)(features)

    wait(ya)
    per = 4 // n_y
    for u in range(per):
        total = GA[core, y * per + u] + RCA[y * per + u].astype(F32)
        for m in range(1, n_y):
            total = total + RYA[m, u].astype(F32)
        total = total.reshape(n_z, rows, W)
        TA[:, u] = total
        ZSA[:, u] = total.astype(BF)
    start(za)

    pl.loop(4, 8, unroll=4)(features)
    for d in (0, 1):
        feat[:, d] = FO[d].reshape(128, 8, W).astype(BF)

    half = rows // 2
    wait(zb)
    total = GB[core, z] + RCB[z].astype(F32)
    for m in range(1, n_z):
        total = total + RZB[m].astype(F32)
    for e in (0, 1):
        YSB[e] = total[:, e * half : (e + 1) * half].astype(BF)
    RYB[y] = YSB[yl]
    start(yb_copies(False))

    wait(za)
    total = TA[z]
    for m in range(1, n_z):
        total = total + RZA[m].astype(F32)
    RXA[dep] = total.astype(BF)
    start(xa_copies(False))

    wait(yb_copies(True))
    total = RYB[0].astype(F32)
    for m in range(1, n_y):
        total = total + RYB[m].astype(F32)
    RXB[core, dep] = total.astype(BF)
    start(xb_copies(False))

    wait(xa_copies(True))
    total = RXA[0].astype(F32)
    for m in range(1, n_dep):
        total = total + RXA[m].astype(F32)
    for e in (0, 1):
        FA[core, y, e] = total[:, e * half : (e + 1) * half]
    start(fa_copies(False))

    wait(xb_copies(True))
    for c in (0, 1):
        total = RXB[c, 0].astype(F32)
        for m in range(1, n_dep):
            total = total + RXB[c, m].astype(F32)
        FB[c] = total
    wait(fa_copies(True))

    def unit_of(owner, unit):
        if unit < 4:
            return FA[owner, unit // per, yl, unit % per]
        return FB[owner, unit - 4]

    for t in range(9):
        got = unit_of(0, t)
        g2_out[3 * t] = got[:, :64]
        g2_out[3 * t + 1] = got[:, 64:]
    taps = [(a, b) for a in range(3) for b in (0, 1)] + [(0, 2), (1, 2), (2, 2)]
    for n, (a, b) in enumerate(taps):
        got = unit_of(1, n // 2)
        g2_out[9 * a + 3 * b + 2] = got[:, (n % 2) * 64 : (n % 2) * 64 + 64]
    own = half // 2
    for block in range(7):
        got = FB[1, 1 + block // 2, (block % 2) * own : (block % 2) * own + own, :]
        for n in range(4 if block < 6 else 3):
            lanes = got[:, n * 32 : n * 32 + 32]
            if block < 6:
                g1_out[3 * (4 * (block % 2) + n) + block // 2] = lanes
            else:
                g1_out[24 + n] = lanes

    for copy in sent + [ca, cb]:
        copy.wait_send()
    halo(near, 1, "wait_send")
    halo(far, 1, "wait_send")
    halo(b_copy, 1, "wait_send")


def write_out(*refs):
    sem = refs[6]
    copies = [pltpu.make_async_copy(refs[n], refs[3 + n], sem.at[n]) for n in range(3)]
    for copy in copies:
        copy.start()
    for copy in copies:
        copy.wait()


def per_device(sizes, volume, kernel_first, kernel_second, cotangent):
    n_z, n_y, n_dep, n_hgt = sizes
    rows, per = 128 // n_z, 4 // n_y
    vmem = pl.BlockSpec(memory_space=pltpu.VMEM)
    dma = pltpu.SemaphoreType.DMA
    results = pl.pallas_call(
        functools.partial(kernel, sizes),
        out_shape=(
            jax.ShapeDtypeStruct((128, 2, 8, W), BF),
            jax.ShapeDtypeStruct((27, rows // 4, 32), F32),
            jax.ShapeDtypeStruct((27, rows // 2, 64), F32),
        ),
        in_specs=[pl.BlockSpec(memory_space=pltpu.HBM)] * 4,
        out_specs=(vmem, vmem, vmem),
        scratch_shapes=[
            pltpu.VMEM((32, 2, 8, W), BF),
            pltpu.VMEM((27, 32, 64), BF),
            pltpu.VMEM((27, 64, 128), BF),
            pltpu.VMEM((128, 2, 8, W), BF),
            pltpu.VMEM((6, 12, 32, W), BF),
            pltpu.VMEM((2, 12, 128, W), BF),
            pltpu.VMEM((1024, W), F32),
            pltpu.VMEM((192, 288), BF),
            pltpu.VMEM((384, 576), BF),
            pltpu.VMEM((576, 384), BF),
            pltpu.VMEM((4, 10, 64, W), BF),
            pltpu.VMEM((2, 10, 64, W), F32),
            pltpu.VMEM((2, 8, 64, W), BF),
            pltpu.VMEM((2, 2, 64, W), BF),
            pltpu.VMEM((4, 64, W), BF),
            pltpu.VMEM((4, 10, 64, W), BF),
            pltpu.VMEM((4, 10, 192, W), BF),
            pltpu.VMEM((2, 10, 64, W), F32),
            pltpu.VMEM((16, 192, W), BF),
            pltpu.VMEM((2, 4, 128, W), F32),
            pltpu.VMEM((2, 4, 128, W), BF),
            pltpu.VMEM((4, 128, W), BF),
            pltpu.VMEM((n_y, per, 128, W), BF),
            pltpu.VMEM((n_y, per, 128, W), BF),
            pltpu.VMEM((n_z, per, rows, W), F32),
            pltpu.VMEM((n_z, per, rows, W), BF),
            pltpu.VMEM((n_z, per, rows, W), BF),
            pltpu.VMEM((n_dep, per, rows, W), BF),
            pltpu.VMEM((2, n_y, 2, per, rows // 2, W), F32),
            pltpu.VMEM((2, n_z, 5, rows, W), F32),
            pltpu.VMEM((2, n_z, 5, rows, W), BF),
            pltpu.VMEM((n_z, 5, rows, W), BF),
            pltpu.VMEM((n_z, 5, rows, W), BF),
            pltpu.VMEM((n_z, 5, rows, W), BF),
            pltpu.VMEM((2, 5, rows // 2, W), BF),
            pltpu.VMEM((n_y, 5, rows // 2, W), BF),
            pltpu.VMEM((2, n_dep, 5, rows // 2, W), BF),
            pltpu.VMEM((2, 5, rows // 2, W), F32),
            pltpu.VMEM((2, 1024, W), F32),
            dma((4,)),
            dma((2, 8)),
            dma((2, 8)),
            dma((8,)),
            dma((8,)),
            dma,
            dma,
            dma((n_y,)),
            dma((n_y,)),
            dma((n_z,)),
            dma((n_z,)),
            dma((n_dep,)),
            dma((n_dep,)),
            dma((2 * n_y,)),
            dma((2 * n_y,)),
            dma,
            dma,
            dma((n_z,)),
            dma((n_z,)),
            dma((n_y,)),
            dma((n_y,)),
            dma((2 * n_dep,)),
            dma((2 * n_dep,)),
        ],
        compiler_params=pltpu.CompilerParams(
            collective_id=0, has_side_effects=True, vmem_limit_bytes=40 * 1024 * 1024
        ),
    )(
        *[
            pltpu.with_memory_space_constraint(x, pltpu.HBM)
            for x in (
                volume[0],
                kernel_first.swapaxes(1, 2),
                kernel_second.swapaxes(1, 2),
                cotangent[0],
            )
        ]
    )
    features, grad_first, grad_second = pl.pallas_call(
        write_out,
        out_shape=tuple(jax.ShapeDtypeStruct(x.shape, x.dtype) for x in results),
        in_specs=[vmem] * 3,
        out_specs=(pl.BlockSpec(memory_space=pltpu.HBM),) * 3,
        scratch_shapes=[dma((3,))],
        compiler_params=pltpu.CompilerParams(vmem_limit_bytes=8 * 1024 * 1024),
    )(*results)
    return features[None], grad_first, grad_second


def solution(mesh):
    placed = (P("dp", None, "dep", "hgt", None), P(), P(), P("dp", None, "dep", "hgt", None))
    shape = mesh.shape
    sizes = (shape["dp"] // 2, shape["hgt"] // 2 * 2, shape["dep"], shape["hgt"])
    return jax.shard_map(
        functools.partial(per_device, sizes),
        mesh=mesh,
        in_specs=placed,
        out_specs=(P("dp", None, "dep", "hgt", None), P(None, "dp", None), P(None, "dp", None)),
        check_vma=False,
    )
```

```python
import functools

import jax
import jax.numpy as jnp
from jax import lax
from jax.experimental import pallas as pl
from jax.experimental.pallas import tpu as pltpu
from jax.sharding import PartitionSpec as P

MESH = pl.DeviceIdType.MESH
BF = jnp.bfloat16
F32 = jnp.float32
W = 128
DIRS = [(a, b) for a in (-1, 0, 1) for b in (-1, 0, 1) if (a, b) != (0, 0)]
NT = (((1,), (1,)), ((), ()))


def dot(a, b):
    return jnp.dot(a, b, preferred_element_type=F32)


def shifted(x, by):
    if by == 0:
        return x
    lane = lax.broadcasted_iota(jnp.int32, x.shape, 1)
    keep = lane >= by if by > 0 else lane < W + by
    return jnp.where(keep, pltpu.roll(x, by % W, 1), 0.0)


def pair(ref, d, h, rows):
    halves = [ref[d + e, pl.ds(h, 3)].reshape(rows, W) for e in (0, 1)]
    return jnp.concatenate(halves, axis=1)


def kernel(
    sizes,
    vol_hbm,
    k1t_hbm,
    k2t_hbm,
    cot_hbm,
    feat,
    g1_out,
    g2_out,
    vol,
    k1t,
    k2t,
    cot,
    V,
    C,
    tmp,
    W1,
    W2,
    WB,
    BO,
    H,
    H3,
    D3,
    PN,
    P1,
    GA,
    GA16,
    RCA,
    YSA,
    RYA,
    TA,
    ZSA,
    RZA,
    YSX,
    RXA,
    FA,
    GB,
    GB16,
    RCB,
    ZSB,
    RZB,
    YSB,
    RYB,
    RXB,
    FB,
    FO,
    in_sem,
    v_send,
    v_recv,
    ca_send,
    ca_recv,
    ya_send,
    ya_recv,
    za_send,
    za_recv,
    xa_send,
    xa_recv,
    cb_send,
    cb_recv,
    zb_send,
    zb_recv,
    yb_send,
    yb_recv,
    xb_send,
    xb_recv,
):
    n_z, n_y, n_dep, n_hgt = sizes
    rows = 128 // n_z
    dp, dep, hgt = (lax.axis_index(name) for name in ("dp", "dep", "hgt"))
    z, yl = dp // 2, dp % 2
    yh, core = hgt // 2, hgt % 2
    y = yh * 2 + yl

    def there(direction, sign):
        d, h = dep + sign * direction[0], hgt + sign * direction[1]
        return (d >= 0) & (d < n_dep) & (h >= 0) & (h < n_hgt)

    def z_peer(m):
        return (((z + m) % n_z) * 2 + yl, dep, hgt)

    def y_peer(m):
        other = (y + m) % n_y
        return (z * 2 + other % 2, dep, (other // 2) * 2 + core)

    def x_peer(m):
        return (dp, (dep + m) % n_dep, hgt)

    def plane_peer(mx, my, far):
        other = (y + my) % n_y
        side = 1 - core if far else core
        return (z * 2 + other % 2, (dep + mx) % n_dep, (other // 2) * 2 + side)

    plane = [
        (mx, my, far)
        for mx in range(n_dep)
        for my in range(n_y)
        for far in (0, 1)
        if mx + my + far > 0
    ]

    partner = (dp, dep, hgt + 1 - 2 * core)

    loads = [
        pltpu.make_async_copy(src, dst, in_sem.at[n])
        for n, (src, dst) in enumerate(
            ((vol_hbm, vol), (cot_hbm, cot), (k2t_hbm, k2t), (k1t_hbm, k1t))
        )
    ]
    for load in loads:
        load.start()

    barrier = pltpu.get_barrier_semaphore()
    peers = [plane_peer(*p) for p in plane] + [z_peer(m) for m in range(1, n_z)]
    for peer in peers:
        pl.semaphore_signal(barrier, inc=1, device_id=peer, device_id_type=MESH)

    for k, (a, b) in enumerate(DIRS):
        rows_d = {0: (2, 4), 1: (0, 2), -1: (4, 6)}[a]
        rows_h = {0: (2, 10), 1: (0, 2), -1: (10, 12)}[b]

        @pl.when(jnp.logical_not(there((a, b), -1)))
        def _():
            block = V.at[rows_d[0] : rows_d[1], rows_h[0] : rows_h[1]]
            block[...] = jnp.zeros(block.shape, BF)

    loads[0].wait()
    for d in (0, 1):
        tmp[0:256, :] = vol[:, d].astype(F32).reshape(256, W)
        for h in range(8):
            V[2 + d, 2 + h] = tmp[pl.ds(h, 32, stride=8), :].astype(BF)

    loads[1].wait()
    for d in (0, 1):
        for h in (0, 1, 10, 11):
            C[d, h] = jnp.zeros((128, W), BF)
        tmp[...] = cot[:, d].astype(F32).reshape(1024, W)

        @pl.loop(0, 8, unroll=4)
        def _(h):
            C[d, 2 + h] = tmp[pl.ds(h, 128, stride=8), :].astype(BF)

    loads[2].wait()
    for a in range(3):
        for b in range(3):
            for c in range(3):
                WB[a * 192 + c * 64 : a * 192 + c * 64 + 64, (2 - b) * 128 : (3 - b) * 128] = k2t[
                    9 * a + 3 * b + c
                ]

    pl.semaphore_wait(barrier, len(peers))

    def v_copy(k, far):
        a, b = DIRS[k]
        from_h, to_h = {0: ((2, 10), (2, 10)), 1: ((8, 10), (0, 2)), -1: ((2, 4), (10, 12))}[b]
        if a == 0:
            src, dst = V.at[2:4, from_h[0] : from_h[1]], V.at[2:4, to_h[0] : to_h[1]]
        else:
            plane = {(1, 0): (3, 1), (1, 1): (2, 0), (-1, 0): (2, 4), (-1, 1): (3, 5)}[a, far]
            src, dst = V.at[plane[0], from_h[0] : from_h[1]], V.at[plane[1], to_h[0] : to_h[1]]
        return pltpu.make_async_remote_copy(
            src_ref=src,
            dst_ref=dst,
            send_sem=v_send.at[far, k],
            recv_sem=v_recv.at[far, k],
            device_id=(dp, dep + a, hgt + b),
            device_id_type=MESH,
        )

    def near(k):
        return v_copy(k, 0)

    def far(k):
        return v_copy(k, 1) if DIRS[k][0] != 0 else None

    def halo(copy, sign, what):
        for k, direction in enumerate(DIRS):

            @pl.when(there(direction, sign))
            def _():
                one = copy(k)
                if one is not None:
                    getattr(one, what)()

    halo(near, 1, "start")
    halo(far, 1, "start")

    @pl.loop(0, 10, unroll=5)
    def _(h):
        t = dot(WB[...], pair(C, 0, h, 384))
        sums = []
        for a in range(3):
            halves = []
            for e in (0, 1):
                parts = [
                    shifted(t[a * 192 + c * 64 : a * 192 + c * 64 + 64, e * W : e * W + W], c - 1)
                    for c in range(3)
                ]
                halves.append(parts[0] + parts[1] + parts[2])
            sums.append(halves)
        BO[0, h] = sums[0][0]
        BO[1, h] = sums[0][1] + sums[1][0]
        BO[2, h] = sums[1][1] + sums[2][0]
        BO[3, h] = sums[2][1]

    loads[3].wait()
    for c in range(3):
        stack = [k1t[3 * t + c].astype(F32) for t in range(9)]
        W1[c * 64 : c * 64 + 64, :] = jnp.concatenate(stack, axis=0).T.astype(BF)

    for c in range(3):
        stack = [k2t[3 * t + c].astype(F32) for t in range(9)]
        W2[c * 128 : c * 128 + 128, :] = jnp.concatenate(stack, axis=0).T.astype(BF)

    halo(near, -1, "wait_recv")

    def hidden(planes):
        def body(h):
            ok_h = ((h > 0) | (hgt > 0)) & ((h < 9) | (hgt < n_hgt - 1))
            x = [
                jnp.concatenate([V[d + a, pl.ds(h, 3)].reshape(96, W) for d in planes], axis=1)
                for a in range(3)
            ]
            t = dot(W1[...], jnp.concatenate(x, axis=0))
            for e, d in enumerate(planes):
                part = [t[c * 64 : c * 64 + 64, e * W : e * W + W] for c in range(3)]
                pre = shifted(part[0], 1) + part[1] + shifted(part[2], -1)
                sigma = 0.5 * jnp.tanh(0.5 * pre) + 0.5
                ok = {0: ok_h & (dep > 0), 3: ok_h & (dep < n_dep - 1)}.get(d, ok_h)
                ok = ok.astype(F32)
                hid = pre * sigma * ok
                delta = BO[d, h] * (sigma * (1.0 + pre * (1.0 - sigma)) * ok)
                H[d, h] = hid.astype(BF)
                for c in range(3):
                    H3[d, h, c * 64 : c * 64 + 64] = shifted(hid, 1 - c).astype(BF)
                    D3[d, h, c * 64 : c * 64 + 64] = shifted(delta, c - 1).astype(BF)

        pl.loop(0, 10, unroll=5)(body)

    def keep(owner, unit, value):
        if unit < 4:
            GA[owner, unit] = value
            GA16[owner, unit] = value.astype(BF)
        else:
            value = value.reshape(n_z, rows, W)
            GB[owner, :, unit - 4] = value
            GB16[owner, :, unit - 4] = value.astype(BF)

    lasts = {}

    def product(left, right):
        left, right = (jnp.concatenate(side, axis=1) for side in (left, right))
        return lax.dot_general(left, right, NT, preferred_element_type=F32)

    def second(a, b, planes):
        return product(
            [C[d, 2 + h] for d in planes for h in range(8)],
            [H3[d + a, h + b] for d in planes for h in range(8)],
        )

    def keep_second(a, b, part):
        keep(0, 3 * a + b, part[:, :128])
        lasts[a, b] = part[:, 128:192]

    def first(planes):
        cells = [(d, h) for d in planes for h in range(10)]
        field = [
            jnp.concatenate([V[d + a, h : h + 3].reshape(96, W) for a in range(3)], axis=0)
            for d, h in cells
        ]
        return product([D3[d, h] for d, h in cells], field)

    hidden((1, 2))
    for b in range(3):
        keep_second(1, b, second(1, b, (0, 1)))
    for n, (a, d) in enumerate(((0, 1), (2, 0))):
        for b in range(3):
            PN[3 * n + b] = second(a, b, (d,))
    P1[...] = first((1, 2))

    halo(far, -1, "wait_recv")
    hidden((0, 3))
    for n, (a, d) in enumerate(((0, 0), (2, 1))):
        for b in range(3):
            keep_second(a, b, second(a, b, (d,)) + PN[3 * n + b])
    for a in range(3):
        keep(1, a, jnp.concatenate([lasts[a, 0], lasts[a, 1]], axis=1))
    keep(1, 3, jnp.concatenate([lasts[0, 2], lasts[1, 2]], axis=1))
    keep(1, 4, jnp.concatenate([lasts[2, 2], jnp.zeros((128, 64), F32)], axis=1))

    def remote(src, dst, send, recv, peer):
        return pltpu.make_async_remote_copy(
            src_ref=src,
            dst_ref=dst,
            send_sem=send,
            recv_sem=recv,
            device_id=peer,
            device_id_type=MESH,
        )

    ca = remote(GA16.at[1 - core], RCA, ca_send, ca_recv, partner)
    cb = remote(GB16.at[1 - core], RCB, cb_send, cb_recv, partner)
    ya = [remote(YSA.at[(y + m) % n_y], RYA.at[m], ya_send.at[m], ya_recv.at[m], y_peer(m)) for m in range(1, n_y)]
    za = [remote(ZSA.at[(z + m) % n_z], RZA.at[m], za_send.at[m], za_recv.at[m], z_peer(m)) for m in range(1, n_z)]
    zb = [remote(ZSB.at[(z + m) % n_z], RZB.at[m], zb_send.at[m], zb_recv.at[m], z_peer(m)) for m in range(1, n_z)]

    def xa_copies(arriving):
        copies = []
        for n, (mx, my, far) in enumerate(plane):
            from_core = 1 - core if arriving and far else core
            from_y = (y + n_y - my) % n_y if arriving else y
            from_x = (dep + n_dep - mx) % n_dep if arriving else dep
            copies.append(
                remote(
                    YSX.at[(y + my) % 2],
                    RXA.at[from_core, from_y, from_x],
                    xa_send.at[n],
                    xa_recv.at[n],
                    plane_peer(mx, my, far),
                )
            )
        return copies

    def xb_copies(arriving):
        copies = []
        for m in range(n_dep):
            for other in (0, 1):
                if m + other > 0:
                    slot = (dep + n_dep - m) % n_dep if arriving else dep
                    half = 1 - core if arriving and other else core
                    copies.append(
                        remote(
                            RXB.at[core, dep],
                            RXB.at[half, slot],
                            xb_send.at[2 * m + other],
                            xb_recv.at[2 * m + other],
                            plane_peer(m, 0, other),
                        )
                    )
        return copies

    def yb_copies(arriving):
        return [
            remote(
                YSB.at[(y + m) % 2],
                RYB.at[(y + n_y - m) % n_y if arriving else y],
                yb_send.at[m],
                yb_recv.at[m],
                y_peer(m),
            )
            for m in range(1, n_y)
        ]

    def start(copies):
        for copy in copies:
            copy.start()

    sent = []

    def wait(copies):
        sent.extend(copies)
        for copy in copies:
            copy.wait_recv()

    ca.start()

    @pl.when(core == 1)
    def _():
        cb.start()

    part = first((0, 3)) + P1[...]
    blocks = [part[c * 64 : c * 64 + 64, j * W : j * W + W] for c in range(3) for j in (0, 1)]
    ends = [part[c * 64 : c * 64 + 64, 256:288] for c in range(3)]
    blocks.append(jnp.concatenate(ends + [jnp.zeros((64, 32), F32)], axis=1))
    blocks.append(jnp.zeros((64, W), F32))
    for m in range(4):
        two = [blocks[2 * m + e].reshape(n_z, rows // 2, W) for e in (0, 1)]
        part = [two[e][:, f * (rows // 4) : (f + 1) * (rows // 4)] for f in (0, 1) for e in (0, 1)]
        value = jnp.concatenate(part, axis=1)
        GB[1, :, 1 + m] = value
        GB16[1, :, 1 + m] = value.astype(BF)

    @pl.when(core == 0)
    def _():
        cb.start()

    ca.wait_recv()
    for j in range(n_y):
        for u in range(4 // n_y):
            unit = j * (4 // n_y) + u
            YSA[j, u] = (GA[core, unit] + RCA[unit].astype(F32)).astype(BF)
    start(ya)
    cb.wait_recv()

    @pl.loop(0, n_z, unroll=4)
    def _(j):
        ZSB[j] = (GB[core, j] + RCB[j].astype(F32)).astype(BF)

    start(zb)

    def features(h):
        x = jnp.concatenate([pair(H, a, h, 192) for a in range(3)], axis=0)
        t = dot(W2[...], x)
        for d in (0, 1):
            part = [t[c * 128 : c * 128 + 128, d * W : d * W + W] for c in range(3)]
            total = shifted(part[0], 1) + part[1] + shifted(part[2], -1)
            FO[d, pl.ds(h, 128, stride=8), :] = total

    pl.loop(0, 4, unroll=4)(features)

    wait(ya)
    per = 4 // n_y
    for u in range(per):
        total = GA[core, y * per + u] + RCA[y * per + u].astype(F32)
        for m in range(1, n_y):
            total = total + RYA[m, u].astype(F32)
        total = total.reshape(n_z, rows, W)
        TA[:, u] = total
        ZSA[:, u] = total.astype(BF)
    start(za)

    pl.loop(4, 8, unroll=4)(features)
    for d in (0, 1):
        feat[:, d] = FO[d].reshape(128, 8, W).astype(BF)

    half = rows // 2
    wait(zb)
    total = GB[core, z] + RCB[z].astype(F32)
    for m in range(1, n_z):
        total = total + RZB[m].astype(F32)
    for e in (0, 1):
        YSB[e] = total[:, e * half : (e + 1) * half].astype(BF)
    RYB[y] = YSB[yl]
    start(yb_copies(False))

    wait(za)
    total = TA[z]
    for m in range(1, n_z):
        total = total + RZA[m].astype(F32)
    for e in (0, 1):
        YSX[e] = total[:, e * half : (e + 1) * half].astype(BF)
    RXA[core, y, dep] = YSX[yl]
    start(xa_copies(False))

    wait(yb_copies(True))
    total = RYB[0].astype(F32)
    for m in range(1, n_y):
        total = total + RYB[m].astype(F32)
    RXB[core, dep] = total.astype(BF)
    start(xb_copies(False))

    wait(xa_copies(True))
    for c in (0, 1):
        for j in range(n_y):
            total = RXA[c, j, 0].astype(F32)
            for m in range(1, n_dep):
                total = total + RXA[c, j, m].astype(F32)
            FA[c, j] = total
    wait(xb_copies(True))
    for c in (0, 1):
        total = RXB[c, 0].astype(F32)
        for m in range(1, n_dep):
            total = total + RXB[c, m].astype(F32)
        FB[c] = total

    def unit_of(owner, unit):
        if unit < 4:
            return FA[owner, unit // per, unit % per]
        return FB[owner, unit - 4]

    for t in range(9):
        got = unit_of(0, t)
        g2_out[3 * t] = got[:, :64]
        g2_out[3 * t + 1] = got[:, 64:]
    taps = [(a, b) for a in range(3) for b in (0, 1)] + [(0, 2), (1, 2), (2, 2)]
    for n, (a, b) in enumerate(taps):
        got = unit_of(1, n // 2)
        g2_out[9 * a + 3 * b + 2] = got[:, (n % 2) * 64 : (n % 2) * 64 + 64]
    own = half // 2
    for block in range(7):
        got = FB[1, 1 + block // 2, (block % 2) * own : (block % 2) * own + own, :]
        for n in range(4 if block < 6 else 3):
            lanes = got[:, n * 32 : n * 32 + 32]
            if block < 6:
                g1_out[3 * (4 * (block % 2) + n) + block // 2] = lanes
            else:
                g1_out[24 + n] = lanes

    for copy in sent + [ca, cb]:
        copy.wait_send()
    halo(near, 1, "wait_send")
    halo(far, 1, "wait_send")


def write_out(*refs):
    sem = refs[6]
    copies = [pltpu.make_async_copy(refs[n], refs[3 + n], sem.at[n]) for n in range(3)]
    for copy in copies:
        copy.start()
    for copy in copies:
        copy.wait()


def per_device(sizes, volume, kernel_first, kernel_second, cotangent):
    n_z, n_y, n_dep, n_hgt = sizes
    rows, per = 128 // n_z, 4 // n_y
    vmem = pl.BlockSpec(memory_space=pltpu.VMEM)
    dma = pltpu.SemaphoreType.DMA
    results = pl.pallas_call(
        functools.partial(kernel, sizes),
        out_shape=(
            jax.ShapeDtypeStruct((128, 2, 8, W), BF),
            jax.ShapeDtypeStruct((27, rows // 4, 32), F32),
            jax.ShapeDtypeStruct((27, rows // 2, 64), F32),
        ),
        in_specs=[pl.BlockSpec(memory_space=pltpu.HBM)] * 4,
        out_specs=(vmem, vmem, vmem),
        scratch_shapes=[
            pltpu.VMEM((32, 2, 8, W), BF),
            pltpu.VMEM((27, 32, 64), BF),
            pltpu.VMEM((27, 64, 128), BF),
            pltpu.VMEM((128, 2, 8, W), BF),
            pltpu.VMEM((6, 12, 32, W), BF),
            pltpu.VMEM((2, 12, 128, W), BF),
            pltpu.VMEM((1024, W), F32),
            pltpu.VMEM((192, 288), BF),
            pltpu.VMEM((384, 576), BF),
            pltpu.VMEM((576, 384), BF),
            pltpu.VMEM((4, 10, 64, W), F32),
            pltpu.VMEM((4, 10, 64, W), BF),
            pltpu.VMEM((4, 10, 192, W), BF),
            pltpu.VMEM((4, 10, 192, W), BF),
            pltpu.VMEM((6, 128, 192), F32),
            pltpu.VMEM((192, 288), F32),
            pltpu.VMEM((2, 4, 128, W), F32),
            pltpu.VMEM((2, 4, 128, W), BF),
            pltpu.VMEM((4, 128, W), BF),
            pltpu.VMEM((n_y, per, 128, W), BF),
            pltpu.VMEM((n_y, per, 128, W), BF),
            pltpu.VMEM((n_z, per, rows, W), F32),
            pltpu.VMEM((n_z, per, rows, W), BF),
            pltpu.VMEM((n_z, per, rows, W), BF),
            pltpu.VMEM((2, per, rows // 2, W), BF),
            pltpu.VMEM((2, n_y, n_dep, per, rows // 2, W), BF),
            pltpu.VMEM((2, n_y, per, rows // 2, W), F32),
            pltpu.VMEM((2, n_z, 5, rows, W), F32),
            pltpu.VMEM((2, n_z, 5, rows, W), BF),
            pltpu.VMEM((n_z, 5, rows, W), BF),
            pltpu.VMEM((n_z, 5, rows, W), BF),
            pltpu.VMEM((n_z, 5, rows, W), BF),
            pltpu.VMEM((2, 5, rows // 2, W), BF),
            pltpu.VMEM((n_y, 5, rows // 2, W), BF),
            pltpu.VMEM((2, n_dep, 5, rows // 2, W), BF),
            pltpu.VMEM((2, 5, rows // 2, W), F32),
            pltpu.VMEM((2, 1024, W), F32),
            dma((4,)),
            dma((2, 8)),
            dma((2, 8)),
            dma,
            dma,
            dma((n_y,)),
            dma((n_y,)),
            dma((n_z,)),
            dma((n_z,)),
            dma((2 * n_y * n_dep,)),
            dma((2 * n_y * n_dep,)),
            dma,
            dma,
            dma((n_z,)),
            dma((n_z,)),
            dma((n_y,)),
            dma((n_y,)),
            dma((2 * n_dep,)),
            dma((2 * n_dep,)),
        ],
        compiler_params=pltpu.CompilerParams(
            collective_id=0, has_side_effects=True, vmem_limit_bytes=40 * 1024 * 1024
        ),
    )(
        *[
            pltpu.with_memory_space_constraint(x, pltpu.HBM)
            for x in (
                volume[0],
                kernel_first.swapaxes(1, 2),
                kernel_second.swapaxes(1, 2),
                cotangent[0],
            )
        ]
    )
    features, grad_first, grad_second = pl.pallas_call(
        write_out,
        out_shape=tuple(jax.ShapeDtypeStruct(x.shape, x.dtype) for x in results),
        in_specs=[vmem] * 3,
        out_specs=(pl.BlockSpec(memory_space=pltpu.HBM),) * 3,
        scratch_shapes=[dma((3,))],
        compiler_params=pltpu.CompilerParams(vmem_limit_bytes=8 * 1024 * 1024),
    )(*results)
    return features[None], grad_first, grad_second


def solution(mesh):
    placed = (P("dp", None, "dep", "hgt", None), P(), P(), P("dp", None, "dep", "hgt", None))
    shape = mesh.shape
    sizes = (shape["dp"] // 2, shape["hgt"] // 2 * 2, shape["dep"], shape["hgt"])
    return jax.shard_map(
        functools.partial(per_device, sizes),
        mesh=mesh,
        in_specs=placed,
        out_specs=(P("dp", None, "dep", "hgt", None), P(None, "dp", None), P(None, "dp", None)),
        check_vma=False,
    )
```

```python
import functools

import jax
import jax.numpy as jnp
from jax import lax
from jax.experimental import pallas as pl
from jax.experimental.pallas import tpu as pltpu
from jax.sharding import PartitionSpec as P

MESH = pl.DeviceIdType.MESH
BF = jnp.bfloat16
F32 = jnp.float32
W = 128
DIRS = [(-1, -1), (-1, 1), (1, -1), (1, 1), (-1, 0), (1, 0), (0, -1), (0, 1)]
NT = (((1,), (1,)), ((), ()))


def dot(a, b):
    return jnp.dot(a, b, preferred_element_type=F32)


def shifted(x, by):
    if by == 0:
        return x
    lane = lax.broadcasted_iota(jnp.int32, x.shape, 1)
    keep = lane >= by if by > 0 else lane < W + by
    return jnp.where(keep, pltpu.roll(x, by % W, 1), 0.0)


def pair(ref, d, h, rows):
    halves = [ref[d + e, pl.ds(h, 3)].reshape(rows, W) for e in (0, 1)]
    return jnp.concatenate(halves, axis=1)


def kernel(
    sizes,
    vol_hbm,
    k1t_hbm,
    k2t_hbm,
    cot_hbm,
    feat,
    g1_out,
    g2_out,
    vol,
    k1t,
    k2t,
    cot,
    V,
    C,
    tmp,
    W1,
    W2,
    WB,
    BO,
    H,
    H3,
    D3,
    PN,
    P1,
    GA,
    GA16,
    RCA,
    YSA,
    RYA,
    TA,
    ZSA,
    RZA,
    YSX,
    RXA,
    FA,
    GB,
    GB16,
    RCB,
    ZSB,
    RZB,
    YSB,
    RYB,
    RXB,
    FB,
    FO,
    in_sem,
    v_send,
    v_recv,
    ca_send,
    ca_recv,
    ya_send,
    ya_recv,
    za_send,
    za_recv,
    xa_send,
    xa_recv,
    cb_send,
    cb_recv,
    zb_send,
    zb_recv,
    yb_send,
    yb_recv,
    xb_send,
    xb_recv,
):
    n_z, n_y, n_dep, n_hgt = sizes
    rows = 128 // n_z
    dp, dep, hgt = (lax.axis_index(name) for name in ("dp", "dep", "hgt"))
    z, yl = dp // 2, dp % 2
    yh, core = hgt // 2, hgt % 2
    y = yh * 2 + yl

    def there(direction, sign):
        d, h = dep + sign * direction[0], hgt + sign * direction[1]
        return (d >= 0) & (d < n_dep) & (h >= 0) & (h < n_hgt)

    def z_peer(m):
        return (((z + m) % n_z) * 2 + yl, dep, hgt)

    def y_peer(m):
        other = (y + m) % n_y
        return (z * 2 + other % 2, dep, (other // 2) * 2 + core)

    def x_peer(m):
        return (dp, (dep + m) % n_dep, hgt)

    def plane_peer(mx, my, far):
        other = (y + my) % n_y
        side = 1 - core if far else core
        return (z * 2 + other % 2, (dep + mx) % n_dep, (other // 2) * 2 + side)

    plane = [
        (mx, my, far)
        for mx in range(n_dep)
        for my in range(n_y)
        for far in (0, 1)
        if mx + my + far > 0
    ]

    partner = (dp, dep, hgt + 1 - 2 * core)

    loads = [
        pltpu.make_async_copy(src, dst, in_sem.at[n])
        for n, (src, dst) in enumerate(
            ((vol_hbm, vol), (cot_hbm, cot), (k2t_hbm, k2t), (k1t_hbm, k1t))
        )
    ]
    for load in loads:
        load.start()

    barrier = pltpu.get_barrier_semaphore()
    peers = [(min(m, n_z - m), z_peer(m)) for m in range(1, n_z)]
    for mx, my, side in plane:
        peers.append((min(mx, n_dep - mx) + min(my, n_y - my), plane_peer(mx, my, side)))
    peers = [peer for _, peer in sorted(peers, key=lambda entry: -entry[0])]
    for peer in peers:
        pl.semaphore_signal(barrier, inc=1, device_id=peer, device_id_type=MESH)

    for k, (a, b) in enumerate(DIRS):
        rows_d = {0: (2, 4), 1: (0, 2), -1: (4, 6)}[a]
        rows_h = {0: (2, 10), 1: (0, 2), -1: (10, 12)}[b]

        @pl.when(jnp.logical_not(there((a, b), -1)))
        def _():
            block = V.at[rows_d[0] : rows_d[1], rows_h[0] : rows_h[1]]
            block[...] = jnp.zeros(block.shape, BF)

    loads[0].wait()
    for d in (0, 1):
        tmp[0:256, :] = vol[:, d].astype(F32).reshape(256, W)
        for h in range(8):
            V[2 + d, 2 + h] = tmp[pl.ds(h, 32, stride=8), :].astype(BF)

    loads[1].wait()
    for d in (0, 1):
        for h in (0, 1, 10, 11):
            C[d, h] = jnp.zeros((128, W), BF)
        tmp[...] = cot[:, d].astype(F32).reshape(1024, W)

        @pl.loop(0, 8, unroll=4)
        def _(h):
            C[d, 2 + h] = tmp[pl.ds(h, 128, stride=8), :].astype(BF)

    loads[2].wait()
    for a in range(3):
        for b in range(3):
            for c in range(3):
                WB[a * 192 + c * 64 : a * 192 + c * 64 + 64, (2 - b) * 128 : (3 - b) * 128] = k2t[
                    9 * a + 3 * b + c
                ]

    pl.semaphore_wait(barrier, len(peers))

    def v_copy(k, far):
        a, b = DIRS[k]
        from_h, to_h = {0: ((2, 10), (2, 10)), 1: ((8, 10), (0, 2)), -1: ((2, 4), (10, 12))}[b]
        if a == 0:
            src, dst = V.at[2:4, from_h[0] : from_h[1]], V.at[2:4, to_h[0] : to_h[1]]
        else:
            plane = {(1, 0): (3, 1), (1, 1): (2, 0), (-1, 0): (2, 4), (-1, 1): (3, 5)}[a, far]
            src, dst = V.at[plane[0], from_h[0] : from_h[1]], V.at[plane[1], to_h[0] : to_h[1]]
        return pltpu.make_async_remote_copy(
            src_ref=src,
            dst_ref=dst,
            send_sem=v_send.at[far, k],
            recv_sem=v_recv.at[far, k],
            device_id=(dp, dep + a, hgt + b),
            device_id_type=MESH,
        )

    def near(k):
        return v_copy(k, 0)

    def far(k):
        return v_copy(k, 1) if DIRS[k][0] != 0 else None

    def halo(copy, sign, what):
        for k, direction in enumerate(DIRS):

            @pl.when(there(direction, sign))
            def _():
                one = copy(k)
                if one is not None:
                    getattr(one, what)()

    halo(near, 1, "start")

    def back(h):
        t = dot(WB[...], pair(C, 0, h, 384))
        sums = []
        for a in range(3):
            halves = []
            for e in (0, 1):
                parts = [
                    shifted(t[a * 192 + c * 64 : a * 192 + c * 64 + 64, e * W : e * W + W], c - 1)
                    for c in range(3)
                ]
                halves.append(parts[0] + parts[1] + parts[2])
            sums.append(halves)
        BO[0, h] = sums[0][0]
        BO[1, h] = sums[0][1] + sums[1][0]
        BO[2, h] = sums[1][1] + sums[2][0]
        BO[3, h] = sums[2][1]

    pl.loop(0, 5, unroll=5)(back)
    halo(far, 1, "start")
    pl.loop(5, 10, unroll=10 - 5)(back)
    loads[3].wait()
    for c in range(3):
        stack = [k1t[3 * t + c].astype(F32) for t in range(9)]
        W1[c * 64 : c * 64 + 64, :] = jnp.concatenate(stack, axis=0).T.astype(BF)

    for c in range(3):
        stack = [k2t[3 * t + c].astype(F32) for t in range(9)]
        W2[c * 128 : c * 128 + 128, :] = jnp.concatenate(stack, axis=0).T.astype(BF)

    halo(near, -1, "wait_recv")

    def hidden(planes):
        def body(h):
            ok_h = ((h > 0) | (hgt > 0)) & ((h < 9) | (hgt < n_hgt - 1))
            x = [
                jnp.concatenate([V[d + a, pl.ds(h, 3)].reshape(96, W) for d in planes], axis=1)
                for a in range(3)
            ]
            t = dot(W1[...], jnp.concatenate(x, axis=0))
            for e, d in enumerate(planes):
                part = [t[c * 64 : c * 64 + 64, e * W : e * W + W] for c in range(3)]
                pre = shifted(part[0], 1) + part[1] + shifted(part[2], -1)
                sigma = 0.5 * jnp.tanh(0.5 * pre) + 0.5
                ok = {0: ok_h & (dep > 0), 3: ok_h & (dep < n_dep - 1)}.get(d, ok_h)
                ok = ok.astype(F32)
                hid = pre * sigma * ok
                delta = BO[d, h] * (sigma * (1.0 + pre * (1.0 - sigma)) * ok)
                H[d, h] = hid.astype(BF)
                for c in range(3):
                    H3[d, h, c * 64 : c * 64 + 64] = shifted(hid, 1 - c).astype(BF)
                    D3[d, h, c * 64 : c * 64 + 64] = shifted(delta, c - 1).astype(BF)

        pl.loop(0, 10, unroll=5)(body)

    def keep(owner, unit, value):
        if unit < 4:
            GA[owner, unit] = value
            GA16[owner, unit] = value.astype(BF)
        else:
            value = value.reshape(n_z, rows, W)
            GB[owner, :, unit - 4] = value
            GB16[owner, :, unit - 4] = value.astype(BF)

    lasts = {}

    def product(left, right):
        left, right = (jnp.concatenate(side, axis=1) for side in (left, right))
        return lax.dot_general(left, right, NT, preferred_element_type=F32)

    def second(a, b, planes):
        return product(
            [C[d, 2 + h] for d in planes for h in range(8)],
            [H3[d + a, h + b] for d in planes for h in range(8)],
        )

    def keep_second(a, b, part):
        keep(0, 3 * a + b, part[:, :128])
        lasts[a, b] = part[:, 128:192]

    def first(planes):
        cells = [(d, h) for d in planes for h in range(10)]
        field = [
            jnp.concatenate([V[d + a, h : h + 3].reshape(96, W) for a in range(3)], axis=0)
            for d, h in cells
        ]
        return product([D3[d, h] for d, h in cells], field)

    hidden((1, 2))
    for b in range(3):
        keep_second(1, b, second(1, b, (0, 1)))
    for n, (a, d) in enumerate(((0, 1), (2, 0))):
        for b in range(3):
            PN[3 * n + b] = second(a, b, (d,))
    P1[...] = first((1, 2))

    halo(far, -1, "wait_recv")
    hidden((0, 3))
    for n, (a, d) in enumerate(((0, 0), (2, 1))):
        for b in range(3):
            keep_second(a, b, second(a, b, (d,)) + PN[3 * n + b])
    for a in range(3):
        keep(1, a, jnp.concatenate([lasts[a, 0], lasts[a, 1]], axis=1))
    keep(1, 3, jnp.concatenate([lasts[0, 2], lasts[1, 2]], axis=1))
    keep(1, 4, jnp.concatenate([lasts[2, 2], jnp.zeros((128, 64), F32)], axis=1))

    def remote(src, dst, send, recv, peer):
        return pltpu.make_async_remote_copy(
            src_ref=src,
            dst_ref=dst,
            send_sem=send,
            recv_sem=recv,
            device_id=peer,
            device_id_type=MESH,
        )

    ca = remote(GA16.at[1 - core], RCA, ca_send, ca_recv, partner)
    cb = remote(GB16.at[1 - core], RCB, cb_send, cb_recv, partner)
    ya = [remote(YSA.at[(y + m) % n_y], RYA.at[m], ya_send.at[m], ya_recv.at[m], y_peer(m)) for m in range(1, n_y)]
    za = [remote(ZSA.at[(z + m) % n_z], RZA.at[m], za_send.at[m], za_recv.at[m], z_peer(m)) for m in range(1, n_z)]
    zb = [remote(ZSB.at[(z + m) % n_z], RZB.at[m], zb_send.at[m], zb_recv.at[m], z_peer(m)) for m in range(1, n_z)]

    def xa_copies(arriving):
        copies = []
        for n, (mx, my, far) in enumerate(plane):
            from_core = 1 - core if arriving and far else core
            from_y = (y + n_y - my) % n_y if arriving else y
            from_x = (dep + n_dep - mx) % n_dep if arriving else dep
            copies.append(
                remote(
                    YSX.at[(y + my) % 2],
                    RXA.at[from_core, from_y, from_x],
                    xa_send.at[n],
                    xa_recv.at[n],
                    plane_peer(mx, my, far),
                )
            )
        return copies

    def xb_copies(arriving):
        copies = []
        for m in range(n_dep):
            for other in (0, 1):
                if m + other > 0:
                    slot = (dep + n_dep - m) % n_dep if arriving else dep
                    half = 1 - core if arriving and other else core
                    copies.append(
                        remote(
                            RXB.at[core, dep],
                            RXB.at[half, slot],
                            xb_send.at[2 * m + other],
                            xb_recv.at[2 * m + other],
                            plane_peer(m, 0, other),
                        )
                    )
        return copies

    def yb_copies(arriving):
        return [
            remote(
                YSB.at[(y + m) % 2],
                RYB.at[(y + n_y - m) % n_y if arriving else y],
                yb_send.at[m],
                yb_recv.at[m],
                y_peer(m),
            )
            for m in range(1, n_y)
        ]

    def start(copies):
        for copy in copies:
            copy.start()

    sent = []

    def wait(copies):
        sent.extend(copies)
        for copy in copies:
            copy.wait_recv()

    ca.start()

    @pl.when(core == 1)
    def _():
        cb.start()

    part = first((0, 3)) + P1[...]
    blocks = [part[c * 64 : c * 64 + 64, j * W : j * W + W] for c in range(3) for j in (0, 1)]
    ends = [part[c * 64 : c * 64 + 64, 256:288] for c in range(3)]
    blocks.append(jnp.concatenate(ends + [jnp.zeros((64, 32), F32)], axis=1))
    blocks.append(jnp.zeros((64, W), F32))
    for m in range(4):
        two = [blocks[2 * m + e].reshape(n_z, rows // 2, W) for e in (0, 1)]
        part = [two[e][:, f * (rows // 4) : (f + 1) * (rows // 4)] for f in (0, 1) for e in (0, 1)]
        value = jnp.concatenate(part, axis=1)
        GB[1, :, 1 + m] = value
        GB16[1, :, 1 + m] = value.astype(BF)

    @pl.when(core == 0)
    def _():
        cb.start()

    ca.wait_recv()
    for j in range(n_y):
        for u in range(4 // n_y):
            unit = j * (4 // n_y) + u
            YSA[j, u] = (GA[core, unit] + RCA[unit].astype(F32)).astype(BF)
    start(ya)
    cb.wait_recv()

    @pl.loop(0, n_z, unroll=4)
    def _(j):
        ZSB[j] = (GB[core, j] + RCB[j].astype(F32)).astype(BF)

    start(zb)

    def features(h):
        x = jnp.concatenate([pair(H, a, h, 192) for a in range(3)], axis=0)
        t = dot(W2[...], x)
        for d in (0, 1):
            part = [t[c * 128 : c * 128 + 128, d * W : d * W + W] for c in range(3)]
            total = shifted(part[0], 1) + part[1] + shifted(part[2], -1)
            FO[d, pl.ds(h, 128, stride=8), :] = total

    pl.loop(0, 4, unroll=4)(features)

    wait(ya)
    per = 4 // n_y
    for u in range(per):
        total = GA[core, y * per + u] + RCA[y * per + u].astype(F32)
        for m in range(1, n_y):
            total = total + RYA[m, u].astype(F32)
        total = total.reshape(n_z, rows, W)
        TA[:, u] = total
        ZSA[:, u] = total.astype(BF)
    start(za)

    pl.loop(4, 8, unroll=4)(features)
    for d in (0, 1):
        feat[:, d] = FO[d].reshape(128, 8, W).astype(BF)

    half = rows // 2
    wait(zb)
    total = GB[core, z] + RCB[z].astype(F32)
    for m in range(1, n_z):
        total = total + RZB[m].astype(F32)
    for e in (0, 1):
        YSB[e] = total[:, e * half : (e + 1) * half].astype(BF)
    RYB[y] = YSB[yl]
    start(yb_copies(False))

    wait(za)
    total = TA[z]
    for m in range(1, n_z):
        total = total + RZA[m].astype(F32)
    for e in (0, 1):
        YSX[e] = total[:, e * half : (e + 1) * half].astype(BF)
    RXA[core, y, dep] = YSX[yl]
    start(xa_copies(False))

    wait(yb_copies(True))
    total = RYB[0].astype(F32)
    for m in range(1, n_y):
        total = total + RYB[m].astype(F32)
    RXB[core, dep] = total.astype(BF)
    start(xb_copies(False))

    wait(xa_copies(True))
    for c in (0, 1):
        for j in range(n_y):
            total = RXA[c, j, 0].astype(F32)
            for m in range(1, n_dep):
                total = total + RXA[c, j, m].astype(F32)
            FA[c, j] = total
    wait(xb_copies(True))
    for c in (0, 1):
        total = RXB[c, 0].astype(F32)
        for m in range(1, n_dep):
            total = total + RXB[c, m].astype(F32)
        FB[c] = total

    def unit_of(owner, unit):
        if unit < 4:
            return FA[owner, unit // per, unit % per]
        return FB[owner, unit - 4]

    for t in range(9):
        got = unit_of(0, t)
        g2_out[3 * t] = got[:, :64]
        g2_out[3 * t + 1] = got[:, 64:]
    taps = [(a, b) for a in range(3) for b in (0, 1)] + [(0, 2), (1, 2), (2, 2)]
    for n, (a, b) in enumerate(taps):
        got = unit_of(1, n // 2)
        g2_out[9 * a + 3 * b + 2] = got[:, (n % 2) * 64 : (n % 2) * 64 + 64]
    own = half // 2
    for block in range(7):
        got = FB[1, 1 + block // 2, (block % 2) * own : (block % 2) * own + own, :]
        for n in range(4 if block < 6 else 3):
            lanes = got[:, n * 32 : n * 32 + 32]
            if block < 6:
                g1_out[3 * (4 * (block % 2) + n) + block // 2] = lanes
            else:
                g1_out[24 + n] = lanes

    for copy in sent + [ca, cb]:
        copy.wait_send()
    halo(near, 1, "wait_send")
    halo(far, 1, "wait_send")


def write_out(*refs):
    sem = refs[6]
    copies = [pltpu.make_async_copy(refs[n], refs[3 + n], sem.at[n]) for n in range(3)]
    for copy in copies:
        copy.start()
    for copy in copies:
        copy.wait()


def per_device(sizes, volume, kernel_first, kernel_second, cotangent):
    n_z, n_y, n_dep, n_hgt = sizes
    rows, per = 128 // n_z, 4 // n_y
    vmem = pl.BlockSpec(memory_space=pltpu.VMEM)
    dma = pltpu.SemaphoreType.DMA
    results = pl.pallas_call(
        functools.partial(kernel, sizes),
        out_shape=(
            jax.ShapeDtypeStruct((128, 2, 8, W), BF),
            jax.ShapeDtypeStruct((27, rows // 4, 32), F32),
            jax.ShapeDtypeStruct((27, rows // 2, 64), F32),
        ),
        in_specs=[pl.BlockSpec(memory_space=pltpu.HBM)] * 4,
        out_specs=(vmem, vmem, vmem),
        scratch_shapes=[
            pltpu.VMEM((32, 2, 8, W), BF),
            pltpu.VMEM((27, 32, 64), BF),
            pltpu.VMEM((27, 64, 128), BF),
            pltpu.VMEM((128, 2, 8, W), BF),
            pltpu.VMEM((6, 12, 32, W), BF),
            pltpu.VMEM((2, 12, 128, W), BF),
            pltpu.VMEM((1024, W), F32),
            pltpu.VMEM((192, 288), BF),
            pltpu.VMEM((384, 576), BF),
            pltpu.VMEM((576, 384), BF),
            pltpu.VMEM((4, 10, 64, W), F32),
            pltpu.VMEM((4, 10, 64, W), BF),
            pltpu.VMEM((4, 10, 192, W), BF),
            pltpu.VMEM((4, 10, 192, W), BF),
            pltpu.VMEM((6, 128, 192), F32),
            pltpu.VMEM((192, 288), F32),
            pltpu.VMEM((2, 4, 128, W), F32),
            pltpu.VMEM((2, 4, 128, W), BF),
            pltpu.VMEM((4, 128, W), BF),
            pltpu.VMEM((n_y, per, 128, W), BF),
            pltpu.VMEM((n_y, per, 128, W), BF),
            pltpu.VMEM((n_z, per, rows, W), F32),
            pltpu.VMEM((n_z, per, rows, W), BF),
            pltpu.VMEM((n_z, per, rows, W), BF),
            pltpu.VMEM((2, per, rows // 2, W), BF),
            pltpu.VMEM((2, n_y, n_dep, per, rows // 2, W), BF),
            pltpu.VMEM((2, n_y, per, rows // 2, W), F32),
            pltpu.VMEM((2, n_z, 5, rows, W), F32),
            pltpu.VMEM((2, n_z, 5, rows, W), BF),
            pltpu.VMEM((n_z, 5, rows, W), BF),
            pltpu.VMEM((n_z, 5, rows, W), BF),
            pltpu.VMEM((n_z, 5, rows, W), BF),
            pltpu.VMEM((2, 5, rows // 2, W), BF),
            pltpu.VMEM((n_y, 5, rows // 2, W), BF),
            pltpu.VMEM((2, n_dep, 5, rows // 2, W), BF),
            pltpu.VMEM((2, 5, rows // 2, W), F32),
            pltpu.VMEM((2, 1024, W), F32),
            dma((4,)),
            dma((2, 8)),
            dma((2, 8)),
            dma,
            dma,
            dma((n_y,)),
            dma((n_y,)),
            dma((n_z,)),
            dma((n_z,)),
            dma((2 * n_y * n_dep,)),
            dma((2 * n_y * n_dep,)),
            dma,
            dma,
            dma((n_z,)),
            dma((n_z,)),
            dma((n_y,)),
            dma((n_y,)),
            dma((2 * n_dep,)),
            dma((2 * n_dep,)),
        ],
        compiler_params=pltpu.CompilerParams(
            collective_id=0, has_side_effects=True, vmem_limit_bytes=40 * 1024 * 1024
        ),
    )(
        *[
            pltpu.with_memory_space_constraint(x, pltpu.HBM)
            for x in (
                volume[0],
                kernel_first.swapaxes(1, 2),
                kernel_second.swapaxes(1, 2),
                cotangent[0],
            )
        ]
    )
    features, grad_first, grad_second = pl.pallas_call(
        write_out,
        out_shape=tuple(jax.ShapeDtypeStruct(x.shape, x.dtype) for x in results),
        in_specs=[vmem] * 3,
        out_specs=(pl.BlockSpec(memory_space=pltpu.HBM),) * 3,
        scratch_shapes=[dma((3,))],
        compiler_params=pltpu.CompilerParams(vmem_limit_bytes=8 * 1024 * 1024),
    )(*results)
    return features[None], grad_first, grad_second


def solution(mesh):
    placed = (P("dp", None, "dep", "hgt", None), P(), P(), P("dp", None, "dep", "hgt", None))
    shape = mesh.shape
    sizes = (shape["dp"] // 2, shape["hgt"] // 2 * 2, shape["dep"], shape["hgt"])
    return jax.shard_map(
        functools.partial(per_device, sizes),
        mesh=mesh,
        in_specs=placed,
        out_specs=(P("dp", None, "dep", "hgt", None), P(None, "dp", None), P(None, "dp", None)),
        check_vma=False,
    )
```

```python
import functools

import jax
import jax.numpy as jnp
from jax import lax
from jax.experimental import pallas as pl
from jax.experimental.pallas import tpu as pltpu
from jax.sharding import PartitionSpec as P

MESH = pl.DeviceIdType.MESH
BF = jnp.bfloat16
F32 = jnp.float32
W = 128
DIRS = [(-1, -1), (-1, 1), (1, -1), (1, 1), (-1, 0), (1, 0), (0, -1), (0, 1)]
NT = (((1,), (1,)), ((), ()))


def dot(a, b):
    return jnp.dot(a, b, preferred_element_type=F32)


def shifted(x, by):
    if by == 0:
        return x
    lane = lax.broadcasted_iota(jnp.int32, x.shape, 1)
    keep = lane >= by if by > 0 else lane < W + by
    return jnp.where(keep, pltpu.roll(x, by % W, 1), 0.0)


def pair(ref, d, h, rows):
    halves = [ref[d + e, pl.ds(h, 3)].reshape(rows, W) for e in (0, 1)]
    return jnp.concatenate(halves, axis=1)


def kernel(
    sizes,
    vol_hbm,
    k1t_hbm,
    k2t_hbm,
    cot_hbm,
    feat,
    g1_out,
    g2_out,
    vol,
    k1t,
    k2t,
    cot,
    V,
    C,
    tmp,
    W1,
    W2,
    WB,
    BO,
    H,
    H3,
    D3,
    PN,
    P1,
    GA,
    GA16,
    RCA,
    YSA,
    RYA,
    TA,
    ZSA,
    RZA,
    YSX,
    RXA,
    FA,
    GB,
    GB16,
    RCB,
    ZSB,
    RZB,
    YSB,
    RYB,
    RXB,
    FB,
    FO,
    in_sem,
    v_send,
    v_recv,
    ca_send,
    ca_recv,
    ya_send,
    ya_recv,
    za_send,
    za_recv,
    xa_send,
    xa_recv,
    cb_send,
    cb_recv,
    zb_send,
    zb_recv,
    yb_send,
    yb_recv,
    xb_send,
    xb_recv,
):
    n_z, n_y, n_dep, n_hgt = sizes
    rows = 128 // n_z
    dp, dep, hgt = (lax.axis_index(name) for name in ("dp", "dep", "hgt"))
    z, yl = dp // 2, dp % 2
    yh, core = hgt // 2, hgt % 2
    y = yh * 2 + yl

    def there(direction, sign):
        d, h = dep + sign * direction[0], hgt + sign * direction[1]
        return (d >= 0) & (d < n_dep) & (h >= 0) & (h < n_hgt)

    def z_peer(m):
        return (((z + m) % n_z) * 2 + yl, dep, hgt)

    def y_peer(m):
        other = (y + m) % n_y
        return (z * 2 + other % 2, dep, (other // 2) * 2 + core)

    def x_peer(m):
        return (dp, (dep + m) % n_dep, hgt)

    def plane_peer(mx, my, far):
        other = (y + my) % n_y
        side = 1 - core if far else core
        return (z * 2 + other % 2, (dep + mx) % n_dep, (other // 2) * 2 + side)

    plane = [
        (mx, my, far)
        for mx in range(n_dep)
        for my in range(n_y)
        for far in (0, 1)
        if mx + my + far > 0
    ]

    partner = (dp, dep, hgt + 1 - 2 * core)

    loads = [
        pltpu.make_async_copy(src, dst, in_sem.at[n])
        for n, (src, dst) in enumerate(
            ((vol_hbm, vol), (cot_hbm, cot), (k2t_hbm, k2t), (k1t_hbm, k1t))
        )
    ]
    for load in loads:
        load.start()

    barrier = pltpu.get_barrier_semaphore()
    peers = [(min(m, n_z - m), z_peer(m)) for m in range(1, n_z)]
    for mx, my, side in plane:
        peers.append((min(mx, n_dep - mx) + min(my, n_y - my), plane_peer(mx, my, side)))
    peers = [peer for _, peer in sorted(peers, key=lambda entry: -entry[0])]
    for peer in peers:
        pl.semaphore_signal(barrier, inc=1, device_id=peer, device_id_type=MESH)

    for k, (a, b) in enumerate(DIRS):
        rows_d = {0: (2, 4), 1: (0, 2), -1: (4, 6)}[a]
        rows_h = {0: (2, 10), 1: (0, 2), -1: (10, 12)}[b]

        @pl.when(jnp.logical_not(there((a, b), -1)))
        def _():
            block = V.at[rows_d[0] : rows_d[1], rows_h[0] : rows_h[1]]
            block[...] = jnp.zeros(block.shape, BF)

    loads[0].wait()
    for d in (0, 1):
        tmp[0:256, :] = vol[:, d].astype(F32).reshape(256, W)
        for h in range(8):
            V[2 + d, 2 + h] = tmp[pl.ds(h, 32, stride=8), :].astype(BF)

    loads[1].wait()
    for d in (0, 1):
        for h in (0, 1, 10, 11):
            C[d, h] = jnp.zeros((128, W), BF)
        tmp[...] = cot[:, d].astype(F32).reshape(1024, W)

        @pl.loop(0, 8, unroll=4)
        def _(h):
            C[d, 2 + h] = tmp[pl.ds(h, 128, stride=8), :].astype(BF)

    loads[2].wait()
    for a in range(3):
        for b in range(3):
            for c in range(3):
                WB[a * 192 + c * 64 : a * 192 + c * 64 + 64, (2 - b) * 128 : (3 - b) * 128] = k2t[
                    9 * a + 3 * b + c
                ]

    pl.semaphore_wait(barrier, len(peers))

    def v_copy(k, far):
        a, b = DIRS[k]
        from_h, to_h = {0: ((2, 10), (2, 10)), 1: ((8, 10), (0, 2)), -1: ((2, 4), (10, 12))}[b]
        if a == 0:
            src, dst = V.at[2:4, from_h[0] : from_h[1]], V.at[2:4, to_h[0] : to_h[1]]
        else:
            plane = {(1, 0): (3, 1), (1, 1): (2, 0), (-1, 0): (2, 4), (-1, 1): (3, 5)}[a, far]
            src, dst = V.at[plane[0], from_h[0] : from_h[1]], V.at[plane[1], to_h[0] : to_h[1]]
        return pltpu.make_async_remote_copy(
            src_ref=src,
            dst_ref=dst,
            send_sem=v_send.at[far, k],
            recv_sem=v_recv.at[far, k],
            device_id=(dp, dep + a, hgt + b),
            device_id_type=MESH,
        )

    def near(k):
        return v_copy(k, 0)

    def far(k):
        return v_copy(k, 1) if DIRS[k][0] != 0 else None

    def halo(copy, sign, what):
        for k, direction in enumerate(DIRS):

            @pl.when(there(direction, sign))
            def _():
                one = copy(k)
                if one is not None:
                    getattr(one, what)()

    halo(near, 1, "start")

    def back(h):
        t = dot(WB[...], pair(C, 0, h, 384))
        sums = []
        for a in range(3):
            halves = []
            for e in (0, 1):
                parts = [
                    shifted(t[a * 192 + c * 64 : a * 192 + c * 64 + 64, e * W : e * W + W], c - 1)
                    for c in range(3)
                ]
                halves.append(parts[0] + parts[1] + parts[2])
            sums.append(halves)
        BO[0, h] = sums[0][0]
        BO[1, h] = sums[0][1] + sums[1][0]
        BO[2, h] = sums[1][1] + sums[2][0]
        BO[3, h] = sums[2][1]

    pl.loop(0, 5, unroll=5)(back)
    halo(far, 1, "start")
    pl.loop(5, 10, unroll=10 - 5)(back)
    loads[3].wait()
    for c in range(3):
        stack = [k1t[3 * t + c].astype(F32) for t in range(9)]
        W1[c * 64 : c * 64 + 64, :] = jnp.concatenate(stack, axis=0).T.astype(BF)

    for c in range(3):
        stack = [k2t[3 * t + c].astype(F32) for t in range(9)]
        W2[c * 128 : c * 128 + 128, :] = jnp.concatenate(stack, axis=0).T.astype(BF)

    halo(near, -1, "wait_recv")

    def hidden(planes):
        def body(h):
            ok_h = ((h > 0) | (hgt > 0)) & ((h < 9) | (hgt < n_hgt - 1))
            x = [
                jnp.concatenate([V[d + a, pl.ds(h, 3)].reshape(96, W) for d in planes], axis=1)
                for a in range(3)
            ]
            t = dot(W1[...], jnp.concatenate(x, axis=0))
            for e, d in enumerate(planes):
                part = [t[c * 64 : c * 64 + 64, e * W : e * W + W] for c in range(3)]
                pre = shifted(part[0], 1) + part[1] + shifted(part[2], -1)
                sigma = 0.5 * jnp.tanh(0.5 * pre) + 0.5
                ok = {0: ok_h & (dep > 0), 3: ok_h & (dep < n_dep - 1)}.get(d, ok_h)
                ok = ok.astype(F32)
                hid = pre * sigma * ok
                delta = BO[d, h] * (sigma * (1.0 + pre * (1.0 - sigma)) * ok)
                H[d, h] = hid.astype(BF)
                for c in range(3):
                    H3[d, h, c * 64 : c * 64 + 64] = shifted(hid, 1 - c).astype(BF)
                    D3[d, h, c * 64 : c * 64 + 64] = shifted(delta, c - 1).astype(BF)

        pl.loop(0, 10, unroll=10)(body)

    def keep(owner, unit, value):
        if unit < 4:
            GA[owner, unit] = value
            GA16[owner, unit] = value.astype(BF)
        else:
            value = value.reshape(n_z, rows, W)
            GB[owner, :, unit - 4] = value
            GB16[owner, :, unit - 4] = value.astype(BF)

    lasts = {}

    def product(left, right):
        left, right = (jnp.concatenate(side, axis=1) for side in (left, right))
        return lax.dot_general(left, right, NT, preferred_element_type=F32)

    def second(a, b, planes):
        return product(
            [C[d, 2 + h] for d in planes for h in range(8)],
            [H3[d + a, h + b] for d in planes for h in range(8)],
        )

    def keep_second(a, b, part):
        keep(0, 3 * a + b, part[:, :128])
        lasts[a, b] = part[:, 128:192]

    def first(planes):
        cells = [(d, h) for d in planes for h in range(10)]
        field = [
            jnp.concatenate([V[d + a, h : h + 3].reshape(96, W) for a in range(3)], axis=0)
            for d, h in cells
        ]
        return product([D3[d, h] for d, h in cells], field)

    hidden((1, 2))
    for b in range(3):
        keep_second(1, b, second(1, b, (0, 1)))
    for n, (a, d) in enumerate(((0, 1), (2, 0))):
        for b in range(3):
            PN[3 * n + b] = second(a, b, (d,))
    P1[...] = first((1, 2))

    halo(far, -1, "wait_recv")
    hidden((0, 3))
    for n, (a, d) in enumerate(((0, 0), (2, 1))):
        for b in range(3):
            keep_second(a, b, second(a, b, (d,)) + PN[3 * n + b])
    for a in range(3):
        keep(1, a, jnp.concatenate([lasts[a, 0], lasts[a, 1]], axis=1))
    keep(1, 3, jnp.concatenate([lasts[0, 2], lasts[1, 2]], axis=1))
    keep(1, 4, jnp.concatenate([lasts[2, 2], jnp.zeros((128, 64), F32)], axis=1))

    def remote(src, dst, send, recv, peer):
        return pltpu.make_async_remote_copy(
            src_ref=src,
            dst_ref=dst,
            send_sem=send,
            recv_sem=recv,
            device_id=peer,
            device_id_type=MESH,
        )

    ca = remote(GA16.at[1 - core], RCA, ca_send, ca_recv, partner)
    cb = remote(GB16.at[1 - core], RCB, cb_send, cb_recv, partner)
    ya = [remote(YSA.at[(y + m) % n_y], RYA.at[m], ya_send.at[m], ya_recv.at[m], y_peer(m)) for m in range(1, n_y)]
    za = [remote(ZSA.at[(z + m) % n_z], RZA.at[m], za_send.at[m], za_recv.at[m], z_peer(m)) for m in range(1, n_z)]
    zb = [remote(ZSB.at[(z + m) % n_z], RZB.at[m], zb_send.at[m], zb_recv.at[m], z_peer(m)) for m in range(1, n_z)]

    def xa_copies(arriving):
        copies = []
        for n, (mx, my, far) in enumerate(plane):
            from_core = 1 - core if arriving and far else core
            from_y = (y + n_y - my) % n_y if arriving else y
            from_x = (dep + n_dep - mx) % n_dep if arriving else dep
            copies.append(
                remote(
                    YSX.at[(y + my) % 2],
                    RXA.at[from_core, from_y, from_x],
                    xa_send.at[n],
                    xa_recv.at[n],
                    plane_peer(mx, my, far),
                )
            )
        return copies

    def xb_copies(arriving):
        copies = []
        for m in range(n_dep):
            for other in (0, 1):
                if m + other > 0:
                    slot = (dep + n_dep - m) % n_dep if arriving else dep
                    half = 1 - core if arriving and other else core
                    copies.append(
                        remote(
                            RXB.at[core, dep],
                            RXB.at[half, slot],
                            xb_send.at[2 * m + other],
                            xb_recv.at[2 * m + other],
                            plane_peer(m, 0, other),
                        )
                    )
        return copies

    def yb_copies(arriving):
        return [
            remote(
                YSB.at[(y + m) % 2],
                RYB.at[(y + n_y - m) % n_y if arriving else y],
                yb_send.at[m],
                yb_recv.at[m],
                y_peer(m),
            )
            for m in range(1, n_y)
        ]

    def start(copies):
        for copy in copies:
            copy.start()

    sent = []

    def wait(copies):
        sent.extend(copies)
        for copy in copies:
            copy.wait_recv()

    ca.start()

    @pl.when(core == 1)
    def _():
        cb.start()

    part = first((0, 3)) + P1[...]
    blocks = [part[c * 64 : c * 64 + 64, j * W : j * W + W] for c in range(3) for j in (0, 1)]
    ends = [part[c * 64 : c * 64 + 64, 256:288] for c in range(3)]
    blocks.append(jnp.concatenate(ends + [jnp.zeros((64, 32), F32)], axis=1))
    blocks.append(jnp.zeros((64, W), F32))
    for m in range(4):
        two = [blocks[2 * m + e].reshape(n_z, rows // 2, W) for e in (0, 1)]
        part = [two[e][:, f * (rows // 4) : (f + 1) * (rows // 4)] for f in (0, 1) for e in (0, 1)]
        value = jnp.concatenate(part, axis=1)
        GB[1, :, 1 + m] = value
        GB16[1, :, 1 + m] = value.astype(BF)

    @pl.when(core == 0)
    def _():
        cb.start()

    ca.wait_recv()
    for j in range(n_y):
        for u in range(4 // n_y):
            unit = j * (4 // n_y) + u
            YSA[j, u] = (GA[core, unit] + RCA[unit].astype(F32)).astype(BF)
    start(ya)
    cb.wait_recv()

    @pl.loop(0, n_z, unroll=4)
    def _(j):
        ZSB[j] = (GB[core, j] + RCB[j].astype(F32)).astype(BF)

    start(zb)

    def features(h):
        x = jnp.concatenate([pair(H, a, h, 192) for a in range(3)], axis=0)
        t = dot(W2[...], x)
        for d in (0, 1):
            part = [t[c * 128 : c * 128 + 128, d * W : d * W + W] for c in range(3)]
            total = shifted(part[0], 1) + part[1] + shifted(part[2], -1)
            FO[d, pl.ds(h, 128, stride=8), :] = total

    pl.loop(0, 4, unroll=4)(features)

    wait(ya)
    per = 4 // n_y
    for u in range(per):
        total = GA[core, y * per + u] + RCA[y * per + u].astype(F32)
        for m in range(1, n_y):
            total = total + RYA[m, u].astype(F32)
        total = total.reshape(n_z, rows, W)
        TA[:, u] = total
        ZSA[:, u] = total.astype(BF)
    start(za)

    pl.loop(4, 8, unroll=4)(features)
    for d in (0, 1):
        feat[:, d] = FO[d].reshape(128, 8, W).astype(BF)

    half = rows // 2
    wait(zb)
    total = GB[core, z] + RCB[z].astype(F32)
    for m in range(1, n_z):
        total = total + RZB[m].astype(F32)
    for e in (0, 1):
        YSB[e] = total[:, e * half : (e + 1) * half].astype(BF)
    RYB[y] = YSB[yl]
    start(yb_copies(False))

    wait(za)
    total = TA[z]
    for m in range(1, n_z):
        total = total + RZA[m].astype(F32)
    for e in (0, 1):
        YSX[e] = total[:, e * half : (e + 1) * half].astype(BF)
    RXA[core, y, dep] = YSX[yl]
    start(xa_copies(False))

    wait(yb_copies(True))
    total = RYB[0].astype(F32)
    for m in range(1, n_y):
        total = total + RYB[m].astype(F32)
    RXB[core, dep] = total.astype(BF)
    start(xb_copies(False))

    wait(xa_copies(True))
    for c in (0, 1):
        for j in range(n_y):
            total = RXA[c, j, 0].astype(F32)
            for m in range(1, n_dep):
                total = total + RXA[c, j, m].astype(F32)
            FA[c, j] = total
    wait(xb_copies(True))
    for c in (0, 1):
        total = RXB[c, 0].astype(F32)
        for m in range(1, n_dep):
            total = total + RXB[c, m].astype(F32)
        FB[c] = total

    def unit_of(owner, unit):
        if unit < 4:
            return FA[owner, unit // per, unit % per]
        return FB[owner, unit - 4]

    for t in range(9):
        got = unit_of(0, t)
        g2_out[3 * t] = got[:, :64]
        g2_out[3 * t + 1] = got[:, 64:]
    taps = [(a, b) for a in range(3) for b in (0, 1)] + [(0, 2), (1, 2), (2, 2)]
    for n, (a, b) in enumerate(taps):
        got = unit_of(1, n // 2)
        g2_out[9 * a + 3 * b + 2] = got[:, (n % 2) * 64 : (n % 2) * 64 + 64]
    own = half // 2
    for block in range(7):
        got = FB[1, 1 + block // 2, (block % 2) * own : (block % 2) * own + own, :]
        for n in range(4 if block < 6 else 3):
            lanes = got[:, n * 32 : n * 32 + 32]
            if block < 6:
                g1_out[3 * (4 * (block % 2) + n) + block // 2] = lanes
            else:
                g1_out[24 + n] = lanes

    for copy in sent + [ca, cb]:
        copy.wait_send()
    halo(near, 1, "wait_send")
    halo(far, 1, "wait_send")


def write_out(*refs):
    sem = refs[6]
    copies = [pltpu.make_async_copy(refs[n], refs[3 + n], sem.at[n]) for n in range(3)]
    for copy in copies:
        copy.start()
    for copy in copies:
        copy.wait()


def per_device(sizes, volume, kernel_first, kernel_second, cotangent):
    n_z, n_y, n_dep, n_hgt = sizes
    rows, per = 128 // n_z, 4 // n_y
    vmem = pl.BlockSpec(memory_space=pltpu.VMEM)
    dma = pltpu.SemaphoreType.DMA
    results = pl.pallas_call(
        functools.partial(kernel, sizes),
        out_shape=(
            jax.ShapeDtypeStruct((128, 2, 8, W), BF),
            jax.ShapeDtypeStruct((27, rows // 4, 32), F32),
            jax.ShapeDtypeStruct((27, rows // 2, 64), F32),
        ),
        in_specs=[pl.BlockSpec(memory_space=pltpu.HBM)] * 4,
        out_specs=(vmem, vmem, vmem),
        scratch_shapes=[
            pltpu.VMEM((32, 2, 8, W), BF),
            pltpu.VMEM((27, 32, 64), BF),
            pltpu.VMEM((27, 64, 128), BF),
            pltpu.VMEM((128, 2, 8, W), BF),
            pltpu.VMEM((6, 12, 32, W), BF),
            pltpu.VMEM((2, 12, 128, W), BF),
            pltpu.VMEM((1024, W), F32),
            pltpu.VMEM((192, 288), BF),
            pltpu.VMEM((384, 576), BF),
            pltpu.VMEM((576, 384), BF),
            pltpu.VMEM((4, 10, 64, W), F32),
            pltpu.VMEM((4, 10, 64, W), BF),
            pltpu.VMEM((4, 10, 192, W), BF),
            pltpu.VMEM((4, 10, 192, W), BF),
            pltpu.VMEM((6, 128, 192), F32),
            pltpu.VMEM((192, 288), F32),
            pltpu.VMEM((2, 4, 128, W), F32),
            pltpu.VMEM((2, 4, 128, W), BF),
            pltpu.VMEM((4, 128, W), BF),
            pltpu.VMEM((n_y, per, 128, W), BF),
            pltpu.VMEM((n_y, per, 128, W), BF),
            pltpu.VMEM((n_z, per, rows, W), F32),
            pltpu.VMEM((n_z, per, rows, W), BF),
            pltpu.VMEM((n_z, per, rows, W), BF),
            pltpu.VMEM((2, per, rows // 2, W), BF),
            pltpu.VMEM((2, n_y, n_dep, per, rows // 2, W), BF),
            pltpu.VMEM((2, n_y, per, rows // 2, W), F32),
            pltpu.VMEM((2, n_z, 5, rows, W), F32),
            pltpu.VMEM((2, n_z, 5, rows, W), BF),
            pltpu.VMEM((n_z, 5, rows, W), BF),
            pltpu.VMEM((n_z, 5, rows, W), BF),
            pltpu.VMEM((n_z, 5, rows, W), BF),
            pltpu.VMEM((2, 5, rows // 2, W), BF),
            pltpu.VMEM((n_y, 5, rows // 2, W), BF),
            pltpu.VMEM((2, n_dep, 5, rows // 2, W), BF),
            pltpu.VMEM((2, 5, rows // 2, W), F32),
            pltpu.VMEM((2, 1024, W), F32),
            dma((4,)),
            dma((2, 8)),
            dma((2, 8)),
            dma,
            dma,
            dma((n_y,)),
            dma((n_y,)),
            dma((n_z,)),
            dma((n_z,)),
            dma((2 * n_y * n_dep,)),
            dma((2 * n_y * n_dep,)),
            dma,
            dma,
            dma((n_z,)),
            dma((n_z,)),
            dma((n_y,)),
            dma((n_y,)),
            dma((2 * n_dep,)),
            dma((2 * n_dep,)),
        ],
        compiler_params=pltpu.CompilerParams(
            collective_id=0, has_side_effects=True, vmem_limit_bytes=40 * 1024 * 1024
        ),
    )(
        *[
            pltpu.with_memory_space_constraint(x, pltpu.HBM)
            for x in (
                volume[0],
                kernel_first.swapaxes(1, 2),
                kernel_second.swapaxes(1, 2),
                cotangent[0],
            )
        ]
    )
    features, grad_first, grad_second = pl.pallas_call(
        write_out,
        out_shape=tuple(jax.ShapeDtypeStruct(x.shape, x.dtype) for x in results),
        in_specs=[vmem] * 3,
        out_specs=(pl.BlockSpec(memory_space=pltpu.HBM),) * 3,
        scratch_shapes=[dma((3,))],
        compiler_params=pltpu.CompilerParams(vmem_limit_bytes=8 * 1024 * 1024),
    )(*results)
    return features[None], grad_first, grad_second


def solution(mesh):
    placed = (P("dp", None, "dep", "hgt", None), P(), P(), P("dp", None, "dep", "hgt", None))
    shape = mesh.shape
    sizes = (shape["dp"] // 2, shape["hgt"] // 2 * 2, shape["dep"], shape["hgt"])
    return jax.shard_map(
        functools.partial(per_device, sizes),
        mesh=mesh,
        in_specs=placed,
        out_specs=(P("dp", None, "dep", "hgt", None), P(None, "dp", None), P(None, "dp", None)),
        check_vma=False,
    )
```

```python
import functools

import jax
import jax.numpy as jnp
from jax import lax
from jax.experimental import pallas as pl
from jax.experimental.pallas import tpu as pltpu
from jax.sharding import PartitionSpec as P

MESH = pl.DeviceIdType.MESH
BF = jnp.bfloat16
F32 = jnp.float32
W = 128
DIRS = [(-1, -1), (-1, 1), (1, -1), (1, 1), (-1, 0), (1, 0), (0, -1), (0, 1)]
NT = (((1,), (1,)), ((), ()))


def dot(a, b):
    return jnp.dot(a, b, preferred_element_type=F32)


def shifted(x, by):
    if by == 0:
        return x
    lane = lax.broadcasted_iota(jnp.int32, x.shape, 1)
    keep = lane >= by if by > 0 else lane < W + by
    return jnp.where(keep, pltpu.roll(x, by % W, 1), 0.0)


def pair(ref, d, h, rows):
    halves = [ref[d + e, pl.ds(h, 3)].reshape(rows, W) for e in (0, 1)]
    return jnp.concatenate(halves, axis=1)


def kernel(
    sizes,
    vol_hbm,
    k1t_hbm,
    k2t_hbm,
    cot_hbm,
    feat,
    g1_out,
    g2_out,
    vol,
    k1t,
    k2t,
    cot,
    V,
    C,
    tmp,
    W1,
    W2,
    WB,
    BO,
    H,
    H3,
    D3,
    PN,
    P1,
    GA,
    GA16,
    RCA,
    YSA,
    RYA,
    TA,
    ZSA,
    RZA,
    YSX,
    RXA,
    FA,
    GB,
    GB16,
    RCB,
    ZSB,
    RZB,
    YSB,
    RYB,
    RXB,
    FB,
    FO,
    in_sem,
    v_send,
    v_recv,
    ca_send,
    ca_recv,
    ya_send,
    ya_recv,
    za_send,
    za_recv,
    xa_send,
    xa_recv,
    cb_send,
    cb_recv,
    zb_send,
    zb_recv,
    yb_send,
    yb_recv,
    xb_send,
    xb_recv,
):
    n_z, n_y, n_dep, n_hgt = sizes
    rows = 128 // n_z
    dp, dep, hgt = (lax.axis_index(name) for name in ("dp", "dep", "hgt"))
    z, yl = dp // 2, dp % 2
    yh, core = hgt // 2, hgt % 2
    y = yh * 2 + yl

    def there(direction, sign):
        d, h = dep + sign * direction[0], hgt + sign * direction[1]
        return (d >= 0) & (d < n_dep) & (h >= 0) & (h < n_hgt)

    def z_peer(m):
        return (((z + m) % n_z) * 2 + yl, dep, hgt)

    def y_peer(m):
        other = (y + m) % n_y
        return (z * 2 + other % 2, dep, (other // 2) * 2 + core)

    def x_peer(m):
        return (dp, (dep + m) % n_dep, hgt)

    def plane_peer(mx, my, far):
        other = (y + my) % n_y
        side = 1 - core if far else core
        return (z * 2 + other % 2, (dep + mx) % n_dep, (other // 2) * 2 + side)

    plane = [
        (mx, my, far)
        for mx in range(n_dep)
        for my in range(n_y)
        for far in (0, 1)
        if mx + my + far > 0
    ]

    partner = (dp, dep, hgt + 1 - 2 * core)

    loads = [
        pltpu.make_async_copy(src, dst, in_sem.at[n])
        for n, (src, dst) in enumerate(
            ((vol_hbm, vol), (cot_hbm, cot), (k2t_hbm, k2t), (k1t_hbm, k1t))
        )
    ]
    for load in loads:
        load.start()

    barrier = pltpu.get_barrier_semaphore()
    peers = [(min(m, n_z - m), z_peer(m)) for m in range(1, n_z)]
    for mx, my, side in plane:
        peers.append((min(mx, n_dep - mx) + min(my, n_y - my), plane_peer(mx, my, side)))
    peers = [peer for _, peer in sorted(peers, key=lambda entry: -entry[0])]
    for peer in peers:
        pl.semaphore_signal(barrier, inc=1, device_id=peer, device_id_type=MESH)

    for k, (a, b) in enumerate(DIRS):
        rows_d = {0: (2, 4), 1: (0, 2), -1: (4, 6)}[a]
        rows_h = {0: (2, 10), 1: (0, 2), -1: (10, 12)}[b]

        @pl.when(jnp.logical_not(there((a, b), -1)))
        def _():
            block = V.at[rows_d[0] : rows_d[1], rows_h[0] : rows_h[1]]
            block[...] = jnp.zeros(block.shape, BF)

    loads[0].wait()
    for d in (0, 1):
        tmp[0:256, :] = vol[:, d].astype(F32).reshape(256, W)
        for h in range(8):
            V[2 + d, 2 + h] = tmp[pl.ds(h, 32, stride=8), :].astype(BF)

    loads[1].wait()
    for d in (0, 1):
        for h in (0, 1, 10, 11):
            C[d, h] = jnp.zeros((128, W), BF)
        tmp[...] = cot[:, d].astype(F32).reshape(1024, W)

        @pl.loop(0, 8, unroll=4)
        def _(h):
            C[d, 2 + h] = tmp[pl.ds(h, 128, stride=8), :].astype(BF)

    loads[2].wait()
    for a in range(3):
        for b in range(3):
            for c in range(3):
                WB[a * 192 + c * 64 : a * 192 + c * 64 + 64, (2 - b) * 128 : (3 - b) * 128] = k2t[
                    9 * a + 3 * b + c
                ]

    pl.semaphore_wait(barrier, len(peers))

    def v_copy(k, far):
        a, b = DIRS[k]
        from_h, to_h = {0: ((2, 10), (2, 10)), 1: ((8, 10), (0, 2)), -1: ((2, 4), (10, 12))}[b]
        if a == 0:
            src, dst = V.at[2:4, from_h[0] : from_h[1]], V.at[2:4, to_h[0] : to_h[1]]
        else:
            plane = {(1, 0): (3, 1), (1, 1): (2, 0), (-1, 0): (2, 4), (-1, 1): (3, 5)}[a, far]
            src, dst = V.at[plane[0], from_h[0] : from_h[1]], V.at[plane[1], to_h[0] : to_h[1]]
        return pltpu.make_async_remote_copy(
            src_ref=src,
            dst_ref=dst,
            send_sem=v_send.at[far, k],
            recv_sem=v_recv.at[far, k],
            device_id=(dp, dep + a, hgt + b),
            device_id_type=MESH,
        )

    def near(k):
        return v_copy(k, 0)

    def far(k):
        return v_copy(k, 1) if DIRS[k][0] != 0 else None

    def halo(copy, sign, what):
        for k, direction in enumerate(DIRS):

            @pl.when(there(direction, sign))
            def _():
                one = copy(k)
                if one is not None:
                    getattr(one, what)()

    halo(near, 1, "start")

    def back(h):
        t = dot(WB[...], pair(C, 0, h, 384))
        sums = []
        for a in range(3):
            halves = []
            for e in (0, 1):
                parts = [
                    shifted(t[a * 192 + c * 64 : a * 192 + c * 64 + 64, e * W : e * W + W], c - 1)
                    for c in range(3)
                ]
                halves.append(parts[0] + parts[1] + parts[2])
            sums.append(halves)
        BO[0, h] = sums[0][0]
        BO[1, h] = sums[0][1] + sums[1][0]
        BO[2, h] = sums[1][1] + sums[2][0]
        BO[3, h] = sums[2][1]

    pl.loop(0, 5, unroll=5)(back)
    halo(far, 1, "start")
    pl.loop(5, 10, unroll=10 - 5)(back)
    loads[3].wait()
    for c in range(3):
        stack = [k1t[3 * t + c].astype(F32) for t in range(9)]
        W1[c * 64 : c * 64 + 64, :] = jnp.concatenate(stack, axis=0).T.astype(BF)

    for c in range(3):
        stack = [k2t[3 * t + c].astype(F32) for t in range(9)]
        W2[c * 128 : c * 128 + 128, :] = jnp.concatenate(stack, axis=0).T.astype(BF)

    halo(near, -1, "wait_recv")

    def hidden(planes):
        def body(h):
            ok_h = {0: hgt > 0, 9: hgt < n_hgt - 1}.get(h)
            x = [
                jnp.concatenate([V[d + a, pl.ds(h, 3)].reshape(96, W) for d in planes], axis=1)
                for a in range(3)
            ]
            t = dot(W1[...], jnp.concatenate(x, axis=0))
            for e, d in enumerate(planes):
                part = [t[c * 64 : c * 64 + 64, e * W : e * W + W] for c in range(3)]
                pre = shifted(part[0], 1) + part[1] + shifted(part[2], -1)
                sigma = 0.5 * jnp.tanh(0.5 * pre) + 0.5
                ok_d = {0: dep > 0, 3: dep < n_dep - 1}.get(d)
                tests = [test for test in (ok_h, ok_d) if test is not None]
                hid = pre * sigma
                delta = BO[d, h] * (sigma * (1.0 + pre * (1.0 - sigma)))
                for test in tests:
                    hid, delta = hid * test.astype(F32), delta * test.astype(F32)
                H[d, h] = hid.astype(BF)
                for c in range(3):
                    H3[d, h, c * 64 : c * 64 + 64] = shifted(hid, 1 - c).astype(BF)
                    D3[d, h, c * 64 : c * 64 + 64] = shifted(delta, c - 1).astype(BF)

        for h in range(10):
            body(h)

    def keep(owner, unit, value):
        if unit < 4:
            GA[owner, unit] = value
            GA16[owner, unit] = value.astype(BF)
        else:
            value = value.reshape(n_z, rows, W)
            GB[owner, :, unit - 4] = value
            GB16[owner, :, unit - 4] = value.astype(BF)

    lasts = {}

    def product(left, right):
        left, right = (jnp.concatenate(side, axis=1) for side in (left, right))
        return lax.dot_general(left, right, NT, preferred_element_type=F32)

    def second(a, b, planes):
        return product(
            [C[d, 2 + h] for d in planes for h in range(8)],
            [H3[d + a, h + b] for d in planes for h in range(8)],
        )

    def keep_second(a, b, part):
        keep(0, 3 * a + b, part[:, :128])
        lasts[a, b] = part[:, 128:192]

    def first(planes):
        cells = [(d, h) for d in planes for h in range(10)]
        field = [
            jnp.concatenate([V[d + a, h : h + 3].reshape(96, W) for a in range(3)], axis=0)
            for d, h in cells
        ]
        return product([D3[d, h] for d, h in cells], field)

    hidden((1, 2))
    for b in range(3):
        keep_second(1, b, second(1, b, (0, 1)))
    for n, (a, d) in enumerate(((0, 1), (2, 0))):
        for b in range(3):
            PN[3 * n + b] = second(a, b, (d,))
    P1[...] = first((1, 2))

    halo(far, -1, "wait_recv")
    hidden((0, 3))
    for n, (a, d) in enumerate(((0, 0), (2, 1))):
        for b in range(3):
            keep_second(a, b, second(a, b, (d,)) + PN[3 * n + b])
    for a in range(3):
        keep(1, a, jnp.concatenate([lasts[a, 0], lasts[a, 1]], axis=1))
    keep(1, 3, jnp.concatenate([lasts[0, 2], lasts[1, 2]], axis=1))
    keep(1, 4, jnp.concatenate([lasts[2, 2], jnp.zeros((128, 64), F32)], axis=1))

    def remote(src, dst, send, recv, peer):
        return pltpu.make_async_remote_copy(
            src_ref=src,
            dst_ref=dst,
            send_sem=send,
            recv_sem=recv,
            device_id=peer,
            device_id_type=MESH,
        )

    ca = remote(GA16.at[1 - core], RCA, ca_send, ca_recv, partner)
    cb = remote(GB16.at[1 - core], RCB, cb_send, cb_recv, partner)
    ya = [remote(YSA.at[(y + m) % n_y], RYA.at[m], ya_send.at[m], ya_recv.at[m], y_peer(m)) for m in range(1, n_y)]
    za = [remote(ZSA.at[(z + m) % n_z], RZA.at[m], za_send.at[m], za_recv.at[m], z_peer(m)) for m in range(1, n_z)]
    zb = [remote(ZSB.at[(z + m) % n_z], RZB.at[m], zb_send.at[m], zb_recv.at[m], z_peer(m)) for m in range(1, n_z)]

    def xa_copies(arriving):
        copies = []
        for n, (mx, my, far) in enumerate(plane):
            from_core = 1 - core if arriving and far else core
            from_y = (y + n_y - my) % n_y if arriving else y
            from_x = (dep + n_dep - mx) % n_dep if arriving else dep
            copies.append(
                remote(
                    YSX.at[(y + my) % 2],
                    RXA.at[from_core, from_y, from_x],
                    xa_send.at[n],
                    xa_recv.at[n],
                    plane_peer(mx, my, far),
                )
            )
        return copies

    def xb_copies(arriving):
        copies = []
        for m in range(n_dep):
            for other in (0, 1):
                if m + other > 0:
                    slot = (dep + n_dep - m) % n_dep if arriving else dep
                    half = 1 - core if arriving and other else core
                    copies.append(
                        remote(
                            RXB.at[core, dep],
                            RXB.at[half, slot],
                            xb_send.at[2 * m + other],
                            xb_recv.at[2 * m + other],
                            plane_peer(m, 0, other),
                        )
                    )
        return copies

    def yb_copies(arriving):
        return [
            remote(
                YSB.at[(y + m) % 2],
                RYB.at[(y + n_y - m) % n_y if arriving else y],
                yb_send.at[m],
                yb_recv.at[m],
                y_peer(m),
            )
            for m in range(1, n_y)
        ]

    def start(copies):
        for copy in copies:
            copy.start()

    sent = []

    def wait(copies):
        sent.extend(copies)
        for copy in copies:
            copy.wait_recv()

    ca.start()

    @pl.when(core == 1)
    def _():
        cb.start()

    part = first((0, 3)) + P1[...]
    blocks = [part[c * 64 : c * 64 + 64, j * W : j * W + W] for c in range(3) for j in (0, 1)]
    ends = [part[c * 64 : c * 64 + 64, 256:288] for c in range(3)]
    blocks.append(jnp.concatenate(ends + [jnp.zeros((64, 32), F32)], axis=1))
    blocks.append(jnp.zeros((64, W), F32))
    for m in range(4):
        two = [blocks[2 * m + e].reshape(n_z, rows // 2, W) for e in (0, 1)]
        part = [two[e][:, f * (rows // 4) : (f + 1) * (rows // 4)] for f in (0, 1) for e in (0, 1)]
        value = jnp.concatenate(part, axis=1)
        GB[1, :, 1 + m] = value
        GB16[1, :, 1 + m] = value.astype(BF)

    @pl.when(core == 0)
    def _():
        cb.start()

    ca.wait_recv()
    for j in range(n_y):
        for u in range(4 // n_y):
            unit = j * (4 // n_y) + u
            YSA[j, u] = (GA[core, unit] + RCA[unit].astype(F32)).astype(BF)
    start(ya)
    cb.wait_recv()

    @pl.loop(0, n_z, unroll=n_z)
    def _(j):
        ZSB[j] = (GB[core, j] + RCB[j].astype(F32)).astype(BF)

    start(zb)

    def features(h):
        x = jnp.concatenate([pair(H, a, h, 192) for a in range(3)], axis=0)
        t = dot(W2[...], x)
        for d in (0, 1):
            part = [t[c * 128 : c * 128 + 128, d * W : d * W + W] for c in range(3)]
            total = shifted(part[0], 1) + part[1] + shifted(part[2], -1)
            FO[d, pl.ds(h, 128, stride=8), :] = total

    pl.loop(0, 4, unroll=4)(features)

    wait(ya)
    per = 4 // n_y
    for u in range(per):
        total = GA[core, y * per + u] + RCA[y * per + u].astype(F32)
        for m in range(1, n_y):
            total = total + RYA[m, u].astype(F32)
        total = total.reshape(n_z, rows, W)
        TA[:, u] = total
        ZSA[:, u] = total.astype(BF)
    start(za)

    pl.loop(4, 8, unroll=4)(features)
    for d in (0, 1):
        feat[:, d] = FO[d].reshape(128, 8, W).astype(BF)

    half = rows // 2
    wait(zb)
    total = GB[core, z] + RCB[z].astype(F32)
    for m in range(1, n_z):
        total = total + RZB[m].astype(F32)
    for e in (0, 1):
        YSB[e] = total[:, e * half : (e + 1) * half].astype(BF)
    RYB[y] = YSB[yl]
    start(yb_copies(False))

    wait(za)
    total = TA[z]
    for m in range(1, n_z):
        total = total + RZA[m].astype(F32)
    for e in (0, 1):
        YSX[e] = total[:, e * half : (e + 1) * half].astype(BF)
    RXA[core, y, dep] = YSX[yl]
    start(xa_copies(False))

    wait(yb_copies(True))
    total = RYB[0].astype(F32)
    for m in range(1, n_y):
        total = total + RYB[m].astype(F32)
    RXB[core, dep] = total.astype(BF)
    start(xb_copies(False))

    wait(xa_copies(True))
    for c in (0, 1):
        for j in range(n_y):
            total = RXA[c, j, 0].astype(F32)
            for m in range(1, n_dep):
                total = total + RXA[c, j, m].astype(F32)
            FA[c, j] = total
    wait(xb_copies(True))
    for c in (0, 1):
        total = RXB[c, 0].astype(F32)
        for m in range(1, n_dep):
            total = total + RXB[c, m].astype(F32)
        FB[c] = total

    def unit_of(owner, unit):
        if unit < 4:
            return FA[owner, unit // per, unit % per]
        return FB[owner, unit - 4]

    for t in range(9):
        got = unit_of(0, t)
        g2_out[3 * t] = got[:, :64]
        g2_out[3 * t + 1] = got[:, 64:]
    taps = [(a, b) for a in range(3) for b in (0, 1)] + [(0, 2), (1, 2), (2, 2)]
    for n, (a, b) in enumerate(taps):
        got = unit_of(1, n // 2)
        g2_out[9 * a + 3 * b + 2] = got[:, (n % 2) * 64 : (n % 2) * 64 + 64]
    own = half // 2
    for block in range(7):
        got = FB[1, 1 + block // 2, (block % 2) * own : (block % 2) * own + own, :]
        for n in range(4 if block < 6 else 3):
            lanes = got[:, n * 32 : n * 32 + 32]
            if block < 6:
                g1_out[3 * (4 * (block % 2) + n) + block // 2] = lanes
            else:
                g1_out[24 + n] = lanes

    for copy in sent + [ca, cb]:
        copy.wait_send()
    halo(near, 1, "wait_send")
    halo(far, 1, "wait_send")


def write_out(*refs):
    sem = refs[6]
    copies = [pltpu.make_async_copy(refs[n], refs[3 + n], sem.at[n]) for n in range(3)]
    for copy in copies:
        copy.start()
    for copy in copies:
        copy.wait()


def per_device(sizes, volume, kernel_first, kernel_second, cotangent):
    n_z, n_y, n_dep, n_hgt = sizes
    rows, per = 128 // n_z, 4 // n_y
    vmem = pl.BlockSpec(memory_space=pltpu.VMEM)
    dma = pltpu.SemaphoreType.DMA
    results = pl.pallas_call(
        functools.partial(kernel, sizes),
        out_shape=(
            jax.ShapeDtypeStruct((128, 2, 8, W), BF),
            jax.ShapeDtypeStruct((27, rows // 4, 32), F32),
            jax.ShapeDtypeStruct((27, rows // 2, 64), F32),
        ),
        in_specs=[pl.BlockSpec(memory_space=pltpu.HBM)] * 4,
        out_specs=(vmem, vmem, vmem),
        scratch_shapes=[
            pltpu.VMEM((32, 2, 8, W), BF),
            pltpu.VMEM((27, 32, 64), BF),
            pltpu.VMEM((27, 64, 128), BF),
            pltpu.VMEM((128, 2, 8, W), BF),
            pltpu.VMEM((6, 12, 32, W), BF),
            pltpu.VMEM((2, 12, 128, W), BF),
            pltpu.VMEM((1024, W), F32),
            pltpu.VMEM((192, 288), BF),
            pltpu.VMEM((384, 576), BF),
            pltpu.VMEM((576, 384), BF),
            pltpu.VMEM((4, 10, 64, W), F32),
            pltpu.VMEM((4, 10, 64, W), BF),
            pltpu.VMEM((4, 10, 192, W), BF),
            pltpu.VMEM((4, 10, 192, W), BF),
            pltpu.VMEM((6, 128, 192), F32),
            pltpu.VMEM((192, 288), F32),
            pltpu.VMEM((2, 4, 128, W), F32),
            pltpu.VMEM((2, 4, 128, W), BF),
            pltpu.VMEM((4, 128, W), BF),
            pltpu.VMEM((n_y, per, 128, W), BF),
            pltpu.VMEM((n_y, per, 128, W), BF),
            pltpu.VMEM((n_z, per, rows, W), F32),
            pltpu.VMEM((n_z, per, rows, W), BF),
            pltpu.VMEM((n_z, per, rows, W), BF),
            pltpu.VMEM((2, per, rows // 2, W), BF),
            pltpu.VMEM((2, n_y, n_dep, per, rows // 2, W), BF),
            pltpu.VMEM((2, n_y, per, rows // 2, W), F32),
            pltpu.VMEM((2, n_z, 5, rows, W), F32),
            pltpu.VMEM((2, n_z, 5, rows, W), BF),
            pltpu.VMEM((n_z, 5, rows, W), BF),
            pltpu.VMEM((n_z, 5, rows, W), BF),
            pltpu.VMEM((n_z, 5, rows, W), BF),
            pltpu.VMEM((2, 5, rows // 2, W), BF),
            pltpu.VMEM((n_y, 5, rows // 2, W), BF),
            pltpu.VMEM((2, n_dep, 5, rows // 2, W), BF),
            pltpu.VMEM((2, 5, rows // 2, W), F32),
            pltpu.VMEM((2, 1024, W), F32),
            dma((4,)),
            dma((2, 8)),
            dma((2, 8)),
            dma,
            dma,
            dma((n_y,)),
            dma((n_y,)),
            dma((n_z,)),
            dma((n_z,)),
            dma((2 * n_y * n_dep,)),
            dma((2 * n_y * n_dep,)),
            dma,
            dma,
            dma((n_z,)),
            dma((n_z,)),
            dma((n_y,)),
            dma((n_y,)),
            dma((2 * n_dep,)),
            dma((2 * n_dep,)),
        ],
        compiler_params=pltpu.CompilerParams(
            collective_id=0, has_side_effects=True, vmem_limit_bytes=40 * 1024 * 1024
        ),
    )(
        *[
            pltpu.with_memory_space_constraint(x, pltpu.HBM)
            for x in (
                volume[0],
                kernel_first.swapaxes(1, 2),
                kernel_second.swapaxes(1, 2),
                cotangent[0],
            )
        ]
    )
    features, grad_first, grad_second = pl.pallas_call(
        write_out,
        out_shape=tuple(jax.ShapeDtypeStruct(x.shape, x.dtype) for x in results),
        in_specs=[vmem] * 3,
        out_specs=(pl.BlockSpec(memory_space=pltpu.HBM),) * 3,
        scratch_shapes=[dma((3,))],
        compiler_params=pltpu.CompilerParams(vmem_limit_bytes=8 * 1024 * 1024),
    )(*results)
    return features[None], grad_first, grad_second


def solution(mesh):
    placed = (P("dp", None, "dep", "hgt", None), P(), P(), P("dp", None, "dep", "hgt", None))
    shape = mesh.shape
    sizes = (shape["dp"] // 2, shape["hgt"] // 2 * 2, shape["dep"], shape["hgt"])
    return jax.shard_map(
        functools.partial(per_device, sizes),
        mesh=mesh,
        in_specs=placed,
        out_specs=(P("dp", None, "dep", "hgt", None), P(None, "dp", None), P(None, "dp", None)),
        check_vma=False,
    )
```
